512 devices in a mesh: sample: 32 (over y, x), space: 16 (over z, core).
Axes of the slice: x: 4, y: 8, z: 8, core: 2. Of those that a mesh axis runs over, the one named last changes fastest.
Arguments:
- input_field: bfloat16 [32, 64, 64, 4, 128], P('sample', None, 'space'), may hold values from -6 to 6
- out_cotangent: bfloat16 [32, 256, 16, 1, 32], P('sample', None, 'space'), may hold values from -6 to 6
- first_weight: bfloat16 [27, 64, 128], replicated, may hold values from -0.15625 to 0.15625
- second_weight: bfloat16 [27, 128, 256], replicated, may hold values from -0.109375 to 0.109375
Outputs:
- input_grad: bfloat16 [32, 64, 64, 4, 128], P('sample', None, 'space')
- first_grad: bfloat16 [27, 64, 128], replicated
- second_grad: bfloat16 [27, 128, 256], P(None, None, 'space')
The draws below stay inside these ranges and needn't reach their ends.
All inputs are finite; a program needn't handle non-finite values.
Results may differ from the reference program's by a relative error of at most 0.008.
Values may be sent and summed in bfloat16 or wider, within the bound.
No kernel may reach another device: no remote copies, remote signals or barrier semaphores. Data moves between devices by JAX's collectives and lax.ppermute only.
A program may use at most 64 MiB of HBM per device.

```python
import math
import jax
import jax.numpy as jnp
from jax import lax

CHAN_IN = 64
CHAN_MID = 128
CHAN_OUT = 256
HEIGHT = 4
LENGTH = 128
SAMPLES = 32
EXTENT = 64


def with_spikes(values, stream_key, source, target, shards_of, factor):
    owner, partner = [(jnp.arange(values.shape[axis_at]) // (values.shape[axis_at] // shards_of)).reshape([-1 if axis == axis_at else 1 for axis in range(values.ndim)]) for axis_at in (source, target)]
    chosen = jax.random.permutation(stream_key, shards_of)[partner]
    strong = (owner == chosen) | (owner == (partner + shards_of // 2) % shards_of)
    return jnp.where(strong, factor * values, values)


def steps_of(stream_key, shape, cuts, least, high):
    def one(dim, parts):
        heights = jax.random.uniform(jax.random.fold_in(jax.random.fold_in(stream_key, 6), dim), (parts,), jnp.float32, least / len(cuts), high / len(cuts))
        return jnp.repeat(jnp.exp(heights), shape[dim] // parts).reshape((-1,) + (1,) * (len(shape) - dim - 1))

    level = one(*cuts[0])
    for cut in cuts[1:]:
        level = level * one(*cut)
    return level


def normal_values(stream_key, shape, scale, reach, cuts=(), held_as=jnp.bfloat16):
    array = jax.random.normal(stream_key, shape, jnp.float32) * scale
    if len(cuts) > 0:
        array = steps_of(stream_key, shape, cuts, -0.22, 0.18) * array
    return jnp.clip(array, min=-reach, max=reach).astype(held_as)


def heavy_noise(stream_key, dims, deviation, bound, cuts, heavy, kind=jnp.bfloat16):
    values = deviation * jax.random.normal(stream_key, dims, jnp.float32)
    if cuts:
        values = values * steps_of(stream_key, dims, cuts, -0.22, 0.18)
    return jnp.clip(with_spikes(values, jax.random.fold_in(stream_key, 3), *heavy), -bound, bound).astype(kind)


def setup_inputs(seed: int = 0) -> dict:
    keys = jax.random.split(jax.random.key(seed), 5)
    input_field = normal_values(keys[0], (SAMPLES, CHAN_IN, EXTENT, HEIGHT, LENGTH), 1.0, 6.0, ((0, 32), (2, 16)))
    out_cotangent = heavy_noise(keys[1], (SAMPLES, CHAN_OUT, EXTENT // 4, HEIGHT // 4, LENGTH // 4), 1.0, 6.0, ((0, 32), (2, 16)), (2, 1, 16, 2.0))
    first_weight = normal_values(keys[2], (27, CHAN_IN, CHAN_MID), (27 * CHAN_IN) ** -0.5, 0.15625)
    second_weight = normal_values(keys[3], (27, CHAN_MID, CHAN_OUT), (27 * CHAN_MID) ** -0.5, 0.109375)
    return {"input_field": input_field, "out_cotangent": out_cotangent, "first_weight": first_weight, "second_weight": second_weight}


def gradient_silu(values):
    logistic = jax.nn.sigmoid(values)
    return logistic * (1.0 + values * (1.0 - logistic))

def parity_split(padded, extents):
    planes_n, rows_n, cells_n = extents
    channels = padded.shape[0]
    grid = jnp.pad(padded, ((0, 0), (0, 1), (0, 1), (0, 1)))
    grid = grid.reshape(channels, planes_n + 1, 2, rows_n + 1, 2, cells_n + 1, 2)
    return grid.transpose(2, 4, 6, 0, 1, 3, 5)

def tap_block(split, extents, offset):
    planes_n, rows_n, cells_n = extents
    slices = []
    for row_tap in range(3):
        for cell_tap in range(3):
            piece = split[offset % 2, row_tap % 2, cell_tap % 2]
            slices.append(piece[:, offset // 2:offset // 2 + planes_n, row_tap // 2:row_tap // 2 + rows_n, cell_tap // 2:cell_tap // 2 + cells_n])
    stacked = jnp.stack(slices, 0)
    return stacked.reshape(-1, planes_n * rows_n * cells_n)

def make_blocks(padded, extents):
    split = parity_split(padded, extents)
    return [tap_block(split, extents, offset) for offset in range(3)]

def apply_filters(blocks, weight):
    channels = weight.shape[1]
    grouped = weight.reshape(3, 9 * channels, weight.shape[2])
    summed = lax.dot_general(grouped[0], blocks[0], (((0,), (0,)), ((), ())), preferred_element_type=jnp.float32)
    for offset in (1, 2):
        summed = summed + lax.dot_general(grouped[offset], blocks[offset], (((0,), (0,)), ((), ())), preferred_element_type=jnp.float32)
    return summed

def filter_gradient(blocks, deltas):
    products = [lax.dot_general(tap_rows, deltas, (((1,), (1,)), ((), ())), preferred_element_type=jnp.float32) for tap_rows in blocks]
    stacked = jnp.stack(products, 0)
    return stacked.reshape(27, -1, deltas.shape[0])

def alternate(taps, spatial):
    leading, central, trailing = (taps[0], taps[1], taps[2])
    planes_in = central.shape[spatial]
    widths = [(0, 0)] * leading.ndim
    upper_pad = list(widths)
    upper_pad[spatial] = (0, 1)
    lower_pad = list(widths)
    lower_pad[spatial] = (1, 0)
    even_part = jnp.pad(leading, upper_pad) + jnp.pad(trailing, lower_pad)
    paired = jnp.stack([lax.slice_in_dim(even_part, 0, planes_in, axis=spatial), central], spatial + 1)
    target = list(central.shape)
    target[spatial] = 2 * planes_in
    merged = paired.reshape(target)
    return jnp.concatenate([merged, lax.slice_in_dim(even_part, planes_in, planes_in + 1, axis=spatial)], spatial)

def spread_back(weight, deltas, extents):
    channels, filters = (weight.shape[1], weight.shape[2])
    flat_weight = weight.reshape(27 * channels, filters)
    patches = jnp.dot(flat_weight, deltas, preferred_element_type=jnp.float32)
    spread = patches.reshape((3, 3, 3, channels) + tuple(extents))
    spread = alternate(spread, 3)
    spread = alternate(spread, 3)
    spread = alternate(spread, 3)
    return spread

def reference(input_field, out_cotangent, first_weight, second_weight):
    chan_in, chan_mid, chan_out = (first_weight.shape[1], first_weight.shape[2], second_weight.shape[2])
    samples_n = input_field.shape[0]
    first_ext = (input_field.shape[2] // 2, input_field.shape[3] // 2, input_field.shape[4] // 2)
    second_ext = (first_ext[0] // 2, first_ext[1] // 2, first_ext[2] // 2)

    def one_sample(running, sample_pair):
        volume, cotangent = sample_pair
        padded = jnp.pad(volume, ((0, 0), (1, 0), (1, 0), (1, 0)))
        first_blocks = make_blocks(padded, first_ext)
        first_pre = apply_filters(first_blocks, first_weight)
        hidden = jax.nn.silu(first_pre).astype(jnp.bfloat16).reshape((chan_mid,) + first_ext)
        hidden_pad = jnp.pad(hidden, ((0, 0), (1, 0), (1, 0), (1, 0)))
        second_blocks = make_blocks(hidden_pad, second_ext)
        second_pre = apply_filters(second_blocks, second_weight)
        second_delta = (cotangent.reshape(chan_out, -1).astype(jnp.float32) * gradient_silu(second_pre)).astype(jnp.bfloat16)
        second_part = filter_gradient(second_blocks, second_delta)
        hidden_grad = spread_back(second_weight, second_delta, second_ext)[:, 1:, 1:, 1:]
        first_delta = (hidden_grad.reshape(chan_mid, -1) * gradient_silu(first_pre)).astype(jnp.bfloat16)
        first_part = filter_gradient(first_blocks, first_delta)
        volume_grad = spread_back(first_weight, first_delta, first_ext)[:, 1:, 1:, 1:].astype(jnp.bfloat16)
        return ((running[0] + first_part, running[1] + second_part), volume_grad)
    start = (jnp.zeros((27, chan_in, chan_mid), jnp.float32), jnp.zeros((27, chan_mid, chan_out), jnp.float32))
    totals, input_grad = lax.scan(one_sample, start, (input_field, out_cotangent))
    first_scale = 1.0 / math.sqrt(samples_n * first_ext[0] * first_ext[1] * first_ext[2])
    second_scale = 1.0 / math.sqrt(samples_n * second_ext[0] * second_ext[1] * second_ext[2])
    return (input_grad, (totals[0] * first_scale).astype(jnp.bfloat16), (totals[1] * second_scale).astype(jnp.bfloat16))
```

```python
import math

import jax
import jax.numpy as jnp
from jax import lax
from jax.sharding import PartitionSpec as P


def shifted(value, axis, steps):
    count = lax.axis_size(axis)
    initial, last = (max(0, -steps), min(count, count - steps))
    return lax.ppermute(value, axis, [(source, source + steps) for source in range(initial, last)])


def gradient_silu(values):
    logistic = jax.nn.sigmoid(values)
    return logistic * (1.0 + values * (1.0 - logistic))


def parity_split(padded, extents):
    planes_n, rows_n, cells_n = extents
    channels = padded.shape[0]
    grid = jnp.pad(padded, ((0, 0), (0, 1), (0, 1), (0, 1)))
    grid = grid.reshape(channels, planes_n + 1, 2, rows_n + 1, 2, cells_n + 1, 2)
    return grid.transpose(2, 4, 6, 0, 1, 3, 5)


def tap_block(split, extents, offset):
    planes_n, rows_n, cells_n = extents
    slices = []
    for row_tap in range(3):
        for cell_tap in range(3):
            piece = split[offset % 2, row_tap % 2, cell_tap % 2]
            slices.append(
                piece[
                    :,
                    offset // 2 : offset // 2 + planes_n,
                    row_tap // 2 : row_tap // 2 + rows_n,
                    cell_tap // 2 : cell_tap // 2 + cells_n,
                ]
            )
    stacked = jnp.stack(slices, 0)
    return stacked.reshape(-1, planes_n * rows_n * cells_n)


def make_blocks(padded, extents):
    split = parity_split(padded, extents)
    return [tap_block(split, extents, offset) for offset in range(3)]


def apply_filters(blocks, weight):
    channels = weight.shape[1]
    grouped = weight.reshape(3, 9 * channels, weight.shape[2])
    summed = lax.dot_general(
        grouped[0], blocks[0], (((0,), (0,)), ((), ())), preferred_element_type=jnp.float32
    )
    for offset in (1, 2):
        summed = summed + lax.dot_general(
            grouped[offset],
            blocks[offset],
            (((0,), (0,)), ((), ())),
            preferred_element_type=jnp.float32,
        )
    return summed


def filter_gradient(blocks, deltas):
    products = [
        lax.dot_general(
            tap_rows, deltas, (((1,), (1,)), ((), ())), preferred_element_type=jnp.float32
        )
        for tap_rows in blocks
    ]
    stacked = jnp.stack(products, 0)
    return stacked.reshape(27, -1, deltas.shape[0])


def alternate(taps, spatial):
    leading, central, trailing = (taps[0], taps[1], taps[2])
    planes_in = central.shape[spatial]
    widths = [(0, 0)] * leading.ndim
    upper_pad = list(widths)
    upper_pad[spatial] = (0, 1)
    lower_pad = list(widths)
    lower_pad[spatial] = (1, 0)
    even_part = jnp.pad(leading, upper_pad) + jnp.pad(trailing, lower_pad)
    paired = jnp.stack(
        [lax.slice_in_dim(even_part, 0, planes_in, axis=spatial), central], spatial + 1
    )
    target = list(central.shape)
    target[spatial] = 2 * planes_in
    merged = paired.reshape(target)
    return jnp.concatenate(
        [merged, lax.slice_in_dim(even_part, planes_in, planes_in + 1, axis=spatial)], spatial
    )


def spread_back(weight, deltas, extents):
    channels, filters = (weight.shape[1], weight.shape[2])
    flat_weight = weight.reshape(27 * channels, filters)
    patches = jnp.dot(flat_weight, deltas, preferred_element_type=jnp.float32)
    spread = patches.reshape((3, 3, 3, channels) + tuple(extents))
    spread = alternate(spread, 3)
    spread = alternate(spread, 3)
    spread = alternate(spread, 3)
    return spread


def shards(input_field, out_cotangent, first_weight, second_weight):
    volume = input_field[0]
    chan_in, planes, height, length = volume.shape
    chan_mid = first_weight.shape[2]
    chan_out = second_weight.shape[2]
    groups = lax.axis_size("space")
    samples_n = lax.axis_size("sample")
    first_ext = (planes // 2, height // 2, length // 2)
    second_ext = (planes // 4, height // 4, length // 4)
    lower_rim = shifted(volume[:, planes - 1 :], "space", 1)
    padded = jnp.pad(jnp.concatenate([lower_rim, volume], 1), ((0, 0), (0, 0), (1, 0), (1, 0)))
    first_blocks = make_blocks(padded, first_ext)
    first_pre = apply_filters(first_blocks, first_weight)
    hidden = jax.nn.silu(first_pre).astype(jnp.bfloat16).reshape((chan_mid,) + first_ext)
    cotangent = out_cotangent[0]
    gathered = lax.all_gather(hidden, "space", axis=1, tiled=True)
    gathered_pad = jnp.pad(gathered, ((0, 0), (1, 0), (1, 0), (1, 0)))
    gathered_ext = (gathered.shape[1] // 2, height // 4, length // 4)
    gathered_blocks = make_blocks(gathered_pad, gathered_ext)
    per_group = chan_out // groups
    own_weight = lax.dynamic_slice_in_dim(
        second_weight, lax.axis_index("space") * per_group, per_group, 2
    )
    own_pre = apply_filters(gathered_blocks, own_weight)
    own_cotangent = lax.all_to_all(
        cotangent, "space", split_axis=0, concat_axis=1, tiled=True
    ).reshape(per_group, -1)
    own_delta = (own_cotangent.astype(jnp.float32) * gradient_silu(own_pre)).astype(jnp.bfloat16)
    second_part = filter_gradient(gathered_blocks, own_delta)
    second_delta = lax.all_to_all(
        own_delta.reshape((per_group,) + gathered_ext),
        "space",
        split_axis=1,
        concat_axis=0,
        tiled=True,
    ).reshape(chan_out, -1)
    second_scale = 1.0 / math.sqrt(
        samples_n * groups * second_ext[0] * second_ext[1] * second_ext[2]
    )
    second_rows = second_part.astype(jnp.bfloat16).reshape(samples_n, -1, 64)
    second_chunk = (chunk_sum(second_rows, "sample") * second_scale).astype(jnp.bfloat16)
    second_total = everywhere(second_chunk, "sample").reshape(second_part.shape)
    grad_pad = spread_back(second_weight, second_delta, second_ext)
    returned = shifted(grad_pad[:, :1, 1:, 1:], "space", -1)
    interior = grad_pad[:, 1:, 1:, 1:]
    hidden_grad = jnp.concatenate([interior[:, :-1], interior[:, -1:] + returned], 1)
    first_delta = (hidden_grad.reshape(chan_mid, -1) * gradient_silu(first_pre)).astype(
        jnp.bfloat16
    )
    first_part = filter_gradient(first_blocks, first_delta)
    first_scale = 1.0 / math.sqrt(samples_n * groups * first_ext[0] * first_ext[1] * first_ext[2])
    first_rows = first_part.astype(jnp.bfloat16).reshape(samples_n, -1, 128)
    first_chunk = chunk_sum(first_rows, "sample").astype(jnp.bfloat16)
    first_sum = jnp.sum(everywhere(first_chunk, "space").astype(jnp.float32), 0)
    first_chunk = (first_sum * first_scale).astype(jnp.bfloat16)
    first_total = everywhere(first_chunk, "sample").reshape(first_part.shape)
    input_pad = spread_back(first_weight, first_delta, first_ext)
    input_back = shifted(input_pad[:, :1, 1:, 1:].astype(jnp.bfloat16), "space", -1).astype(
        jnp.float32
    )
    input_inner = input_pad[:, 1:, 1:, 1:]
    volume_grad = jnp.concatenate([input_inner[:, :-1], input_inner[:, -1:] + input_back], 1)
    input_grad = volume_grad.astype(jnp.bfloat16)[None]
    return (
        input_grad,
        first_total,
        second_total,
    )


def everywhere(value, axis):
    count = lax.axis_size(axis)
    copies = jnp.broadcast_to(value[None], (count,) + value.shape)
    return lax.all_to_all(copies, axis, split_axis=0, concat_axis=0, tiled=True)


def chunk_sum(parts, axis):
    moved = lax.all_to_all(parts, axis, split_axis=0, concat_axis=0, tiled=True)
    return jnp.sum(moved.astype(jnp.float32), 0)


def solution(mesh):
    placed = (
        P("sample", None, "space", None, None),
        P("sample", None, "space", None, None),
        P(),
        P(),
    )
    return jax.shard_map(
        shards,
        mesh=mesh,
        in_specs=placed,
        out_specs=(P("sample", None, "space", None, None), P(), P(None, None, "space")),
        check_vma=False,
    )
```

```python
import math

import jax
import jax.numpy as jnp
import numpy as np
from jax import lax
from jax.experimental import pallas as pl
from jax.experimental.pallas import tpu as pltpu
from jax.sharding import PartitionSpec as P

BF = jnp.bfloat16
F32 = jnp.float32
PADDED_TAPS = 20


def shifted(value, axis, steps):
    count = lax.axis_size(axis)
    initial, last = (max(0, -steps), min(count, count - steps))
    return lax.ppermute(value, axis, [(source, source + steps) for source in range(initial, last)])


def gradient_silu(values):
    logistic = jax.nn.sigmoid(values)
    return logistic * (1.0 + values * (1.0 - logistic))


def dot(left, right):
    return jnp.dot(left, right, preferred_element_type=F32)


def dot_rows(left, right):
    return lax.dot_general(left, right, (((1,), (1,)), ((), ())), preferred_element_type=F32)


def flat(mask, rows):
    return mask.reshape(rows, -1).astype(BF)


def selections(cells, rows):
    half, quarter = cells // 2, cells // 4
    j, n, e, jj, k = np.indices((rows, cells, 3, rows, half))
    down_first = flat((j == jj) & (n == 2 * k + e - 1), rows * cells)
    j, k, e, jj, n = np.indices((rows, half, 3, rows, cells))
    up_first = flat((j == jj) & (n == 2 * k + e - 1), rows * half)
    b, e, m, j, k = np.indices((2, 3, quarter, rows, half))
    down_second = flat((j == b) & (k == 2 * m + e - 1), 6 * quarter)
    a, j, k, aa, b, e, m = np.indices((3, rows, half, 3, 2, 3, quarter))
    send_second = flat((a == aa) & (j == b) & (k == 2 * m + e - 1), 3 * rows * half)
    width = send_second.shape[1]
    send_second = np.pad(send_second, ((0, 0), (0, -width % 128)))
    i, m, ii, b, e, j, k = np.indices((2, quarter, 2, 2, 3, rows, half))
    up_second = flat((i == ii) & (j == b) & (k == 2 * m + e - 1), 2 * quarter)
    chosen = (down_first, up_first, down_second, send_second, up_second)
    return [jnp.asarray(matrix) for matrix in chosen]


def forward_kernel(
    below, own, above, flipped, second_weight, cotangent, down_first, down_second, send_second,
    pre_ref, delta_ref, payload_ref, blocks, taps,
):
    chan_in = own.shape[2]
    group = 9 * chan_in
    cells = own.shape[3]
    first = 0
    for part in (below, own, above):
        planes = part.shape[0]

        def row(r):
            return part[:, r].reshape(planes * chan_in, cells)

        for b in range(3):
            if b == 0:
                picked = dot(row(1), down_first[cells:, :])
            else:
                picked = dot(jnp.concatenate([row(b - 1), row(b + 1)], 1), down_first[...])
            picked = picked.astype(BF)
            for p in range(planes):
                for e in range(3):
                    start = (first + p) * group + (3 * b + e) * chan_in
                    blocks[start : start + chan_in, :] = picked[
                        p * chan_in : (p + 1) * chan_in, e * 128 : (e + 1) * 128
                    ]
        first += planes
    quarter = cotangent.shape[0] // 2
    hiddens = []
    for h in range(5):
        pre = dot(flipped[...], blocks[2 * h * group : (2 * h + 3) * group, :])
        if 1 <= h <= 3:
            pre_ref[h - 1] = pre
        hidden = (pre * jax.nn.sigmoid(pre)).astype(BF)
        hiddens.append(hidden)
        chan = hidden.shape[0]
        picked = dot_rows(down_second[...], hidden).astype(BF)
        for i in range(2):
            a = h - 2 * i
            if 0 <= a <= 2:
                for be in range(6):
                    taps[i * quarter : (i + 1) * quarter, (6 * a + be) * chan : (6 * a + be + 1) * chan] = (
                        picked[be * quarter : (be + 1) * quarter]
                    )
    chan = hiddens[0].shape[0]
    pre = None
    for a in range(3):
        rows = second_weight[(9 * a + 3) * chan : 9 * (a + 1) * chan, :]
        term = dot(taps[:, 6 * a * chan : 6 * (a + 1) * chan], rows)
        pre = term if pre is None else pre + term
    delta = cotangent[...].astype(F32) * gradient_silu(pre)
    delta_ref[...] = delta.T.astype(BF)
    sent = dot(jnp.concatenate(hiddens[:3], 1), send_second[...]).astype(BF)
    width = sent.shape[1]
    payload_ref[:, :width] = sent
    filters = delta.shape[1]
    for q in range(quarter // 8):
        piece = jnp.concatenate([delta[8 * q : 8 * (q + 1)]] * (chan // 8), 0)
        payload_ref[:, width + q * filters : width + (q + 1) * filters] = piece.astype(BF)


def backward_kernel(
    below, own, delta, pre_ref, first_weight, second_weight, up_first, up_second, volume_ref, grad_ref
):
    chan_in, cells = own.shape[2:]
    chan = pre_ref.shape[1]
    spread = dot(delta[...], up_second[...]).astype(BF)
    lanes = spread.shape[1] // 12
    deltas = []
    for h, pairs in enumerate((((1, 0),), ((2, 0), (0, 1)), ((1, 1),))):
        total = None
        for a, i in pairs:
            for be in range(6):
                start = (9 * a + 3 + be) * chan
                term = dot(
                    second_weight[start : start + chan, :],
                    spread[:, (6 * i + be) * lanes : (6 * i + be + 1) * lanes],
                )
                total = term if total is None else total + term
        deltas.append((total * gradient_silu(pre_ref[h])).astype(BF))
    raised = dot(jnp.concatenate(deltas, 0), up_first[...]).astype(BF)
    wide = 2 * cells
    stacks = [
        jnp.concatenate(
            [raised[h * chan : (h + 1) * chan, e * wide : (e + 1) * wide] for e in range(3)], 0
        )
        for h in range(3)
    ]

    def filters(a):
        return [
            jnp.concatenate([first_weight[9 * a + 3 * b + e] for e in range(3)], 1) for b in range(3)
        ]

    totals = {}
    for h, chosen in enumerate(((1, 2), (0, 1, 2), (0,))):
        left = jnp.concatenate(sum([filters(a) for a in chosen], []), 0)
        result = dot(left, stacks[h])
        for place, a in enumerate(chosen):
            p = 2 * h + a - 1
            for b in range(3):
                for j in range(2):
                    r = 2 * j + b - 1
                    if r < 0:
                        continue
                    start = (3 * place + b) * chan_in
                    term = result[start : start + chan_in, j * cells : (j + 1) * cells]
                    totals[p, r] = totals[p, r] + term if (p, r) in totals else term
    for (p, r), total in totals.items():
        volume_ref[p, r] = total.astype(BF)

    def plane(p, r):
        return below[below.shape[0] - 1, r] if p < 0 else own[p, r]

    blank = jnp.zeros((chan_in, cells), BF)
    lefts = []
    for a in range(3):
        for b in range(3):
            pieces = []
            for i in range(2):
                for j in range(2):
                    r = 2 * j + b - 1
                    pieces.append(blank if r < 0 else plane(2 * i + a - 1, r))
            lefts.append(jnp.concatenate(pieces, 1))
    grads = dot_rows(jnp.concatenate(lefts, 0), jnp.concatenate(stacks[:2], 1)).astype(BF)
    for ab in range(9):
        for e in range(3):
            start = (3 * ab + e) * chan_in
            grad_ref[start : start + chan_in, :] = grads[
                ab * chan_in : (ab + 1) * chan_in, e * chan : (e + 1) * chan
            ]
    grad_ref[27 * chan_in :, :] = jnp.zeros((grad_ref.shape[0] - 27 * chan_in, chan), BF)


def exchanged(parts, axis):
    return lax.all_to_all(parts, axis, split_axis=0, concat_axis=0, tiled=True)


def everywhere(value, axis):
    return exchanged(jnp.broadcast_to(value[None], (lax.axis_size(axis),) + value.shape), axis)


def call(kernel, outs, scratch, flops, moved):
    return pl.pallas_call(
        kernel,
        out_shape=outs,
        scratch_shapes=scratch,
        compiler_params=pltpu.CompilerParams(vmem_limit_bytes=40 << 20),
        cost_estimate=pl.CostEstimate(flops=flops, bytes_accessed=moved, transcendentals=0),
    )


def shards(input_field, out_cotangent, first_weight, second_weight):
    chan_in, planes, height, length = input_field.shape[1:]
    chan_mid, chan_out = second_weight.shape[1:]
    groups = lax.axis_size("space")
    samples_n = lax.axis_size("sample")
    rows, half, quarter = (height // 2, length // 2, length // 4)
    own = input_field[0].transpose(1, 2, 0, 3)
    below = shifted(own[1:], "space", 1)
    above = shifted(own, "space", -1)
    cotangent = out_cotangent[0].reshape(chan_out, quarter).T
    cotangent = jnp.concatenate([cotangent, shifted(cotangent, "space", -1)], 0)
    down_first, up_first, down_second, send_second, up_second = selections(length, rows)
    flipped = first_weight.reshape(27 * chan_in, chan_mid).T
    flat_second = second_weight.reshape(27 * chan_mid, chan_out)
    width = send_second.shape[1]
    pre, delta, payload = call(
        forward_kernel,
        (
            jax.ShapeDtypeStruct((3, chan_mid, rows * half), F32),
            jax.ShapeDtypeStruct((chan_out, 2 * quarter), BF),
            jax.ShapeDtypeStruct((chan_mid, width + quarter // 8 * chan_out), BF),
        ),
        [
            pltpu.VMEM((11 * 9 * chan_in, rows * half), BF),
            pltpu.VMEM((2 * quarter, 18 * chan_mid), BF),
        ],
        2_000_000_000,
        6_000_000,
    )(below, own, above, flipped, flat_second, cotangent, down_first, down_second, send_second)
    own_chan = chan_mid // groups
    moved = exchanged(payload.reshape(groups, own_chan, -1), "space")
    volume, first_part = call(
        backward_kernel,
        (
            jax.ShapeDtypeStruct((planes, height, chan_in, length), BF),
            jax.ShapeDtypeStruct((28 * chan_in, chan_mid), BF),
        ),
        [],
        3_000_000_000,
        6_000_000,
    )(below, own, delta, pre, first_weight, flat_second, up_first, up_second)
    input_grad = volume.transpose(2, 0, 1, 3)[None]
    first_moved = exchanged(first_part.reshape(samples_n, -1, chan_mid), "sample")
    first_chunk = jnp.sum(first_moved.astype(F32), 0).astype(BF)
    fields = moved[:, :, : 18 * quarter].reshape(groups, own_chan, 18, quarter)
    fields = fields.transpose(1, 2, 0, 3).reshape(own_chan * 18, groups * quarter)
    deltas = moved[:, :, width:].reshape(groups, 8, quarter // 8, chan_out)
    deltas = deltas.transpose(0, 2, 1, 3).reshape(groups * quarter, chan_out)
    second_part = dot(fields, deltas).astype(BF).reshape(own_chan, 18, chan_out)
    second_part = jnp.pad(second_part, ((0, 0), (0, PADDED_TAPS - 18), (0, 0)))
    second_moved = exchanged(second_part.reshape(samples_n, -1, chan_out), "sample")
    second_ext = planes // 4 * (height // 4) * quarter
    second_scale = 1.0 / math.sqrt(samples_n * groups * second_ext)
    second_chunk = (jnp.sum(second_moved.astype(F32), 0) * second_scale).astype(BF)
    per_group = chan_out // groups
    rows_n = second_chunk.shape[0]
    count = rows_n * per_group
    packed = -(-count // chan_mid)
    second_chunk = second_chunk.reshape(rows_n, groups, per_group).transpose(1, 0, 2)
    second_chunk = jnp.pad(second_chunk.reshape(groups, count), ((0, 0), (0, packed * chan_mid - count)))
    second_chunk = second_chunk.reshape(groups, packed, chan_mid)
    second_chunk = jnp.pad(second_chunk, ((0, 0), (0, -packed % 8), (0, 0)))
    size = first_chunk.shape[0]
    both = jnp.concatenate(
        [jnp.broadcast_to(first_chunk[None], (groups,) + first_chunk.shape), second_chunk], 1
    )
    both = exchanged(both, "space")
    first_ext = planes // 2 * (height // 2) * half
    first_scale = 1.0 / math.sqrt(samples_n * groups * first_ext)
    first_chunk = (jnp.sum(both[:, :size].astype(F32), 0) * first_scale).astype(BF)
    second_chunk = both[:, size : size + packed].reshape(groups * packed, chan_mid)
    final = everywhere(jnp.concatenate([first_chunk, second_chunk], 0), "sample")
    first_grad = final[:, :size].reshape(28, chan_in, chan_mid)[:27]
    second = final[:, size:].reshape(samples_n, groups, packed * chan_mid)[:, :, :count]
    second = second.reshape(samples_n, groups, rows_n, per_group).transpose(0, 2, 1, 3)
    second = second.reshape(own_chan, PADDED_TAPS, groups, per_group)[:, :18]
    second = second.transpose(1, 2, 0, 3).reshape(3, 2, 3, chan_mid, per_group)
    second_grad = jnp.pad(second, ((0, 0), (1, 0), (0, 0), (0, 0), (0, 0)))
    return input_grad, first_grad, second_grad.reshape(27, chan_mid, per_group)


def solution(mesh):
    placed = (
        P("sample", None, "space", None, None),
        P("sample", None, "space", None, None),
        P(),
        P(),
    )
    return jax.shard_map(
        shards,
        mesh=mesh,
        in_specs=placed,
        out_specs=(P("sample", None, "space", None, None), P(), P(None, None, "space")),
        check_vma=False,
    )
```

```python
import math

import jax
import jax.numpy as jnp
from jax import lax
from jax.experimental import pallas as pl
from jax.experimental.pallas import tpu as pltpu
from jax.sharding import PartitionSpec as P

BF = jnp.bfloat16
F32 = jnp.float32


def shifted(value, axis, steps):
    count = lax.axis_size(axis)
    initial, last = (max(0, -steps), min(count, count - steps))
    return lax.ppermute(value, axis, [(source, source + steps) for source in range(initial, last)])


def gradient_silu(values):
    logistic = jax.nn.sigmoid(values)
    return logistic * (1.0 + values * (1.0 - logistic))


def dot(left, right):
    return jnp.dot(left, right, preferred_element_type=F32)


def dot_rows(left, right):
    return lax.dot_general(left, right, (((1,), (1,)), ((), ())), preferred_element_type=F32)


def picker(rows, columns, test):
    r = lax.broadcasted_iota(jnp.int32, (rows, columns), 0)
    c = lax.broadcasted_iota(jnp.int32, (rows, columns), 1)
    return jnp.where(test(r, c), 1.0, 0.0).astype(BF)


def down_first_test(r, c):
    return ((r >> 7) == ((c >> 6) & 1)) & ((r & 127) == 2 * (c & 63) + (c >> 7) - 1)


def up_first_test(r, c):
    return ((r >> 6) == ((c >> 7) & 1)) & ((c & 127) == 2 * (r & 63) + (c >> 8) - 1)


def down_second_test(r, c):
    be = r >> 5
    b = jnp.where(be >= 3, 1, 0)
    return (b == (c >> 6)) & ((c & 63) == 2 * (r & 31) + be - 3 * b - 1)


def up_second_test(r, c):
    ibe = c >> 7
    i = jnp.where(ibe >= 6, 1, 0)
    be = ibe - 6 * i
    b = jnp.where(be >= 3, 1, 0)
    return ((r >> 5) == i) & (b == ((c >> 6) & 1)) & ((c & 63) == 2 * (r & 31) + be - 3 * b - 1)


def reorder_test(r, c):
    return ((r >> 4) == (c & 15)) & ((r & 15) == (c >> 4))


def forward_kernel(
    parity, below, own, above, flipped, second_weight, pre_ref, delta_ref, kept_ref, sent_ref, blocks, taps
):
    chan_in, cells = 64, 128
    group = 9 * chan_in
    down_first = picker(2 * cells, 3 * 128, down_first_test)
    down_second = picker(192, 128, down_second_test)
    first = 0
    for part, planes in ((below, 3), (own, 4), (above, 4)):

        def row(r):
            lines = [
                part[(4 * p + r) * chan_in : (4 * p + r + 1) * chan_in, :] for p in range(planes)
            ]
            return jnp.concatenate(lines, 0)

        for b in range(3):
            if b == 0:
                picked = dot(row(1), down_first[cells:, :])
            else:
                picked = dot(jnp.concatenate([row(b - 1), row(b + 1)], 1), down_first)
            picked = picked.astype(BF)
            for p in range(planes):
                for e in range(3):
                    start = (first + p) * group + (3 * b + e) * chan_in
                    blocks[start : start + chan_in, :] = picked[
                        p * chan_in : (p + 1) * chan_in, e * 128 : (e + 1) * 128
                    ]
        first += planes
    quarter = 32
    lines = 16 * chan_in
    cotangent = jnp.concatenate(
        [
            jnp.concatenate([part[lines : lines + 32, :], part[lines + 32 : lines + 64, :]], 1)
            for part in (own, above)
        ],
        0,
    )
    for h in range(5):
        pre = dot(flipped[...], blocks[2 * h * group : (2 * h + 3) * group, :])
        if 1 <= h <= 3:
            pre_ref[h - 1] = pre
        hidden = (pre * jax.nn.sigmoid(pre)).astype(BF)
        chan = hidden.shape[0]
        picked = dot_rows(down_second, hidden).astype(BF)
        for i in range(2):
            a = h - 2 * i
            if 0 <= a <= 2:
                for be in range(6):
                    taps[i * quarter : (i + 1) * quarter, (6 * a + be) * chan : (6 * a + be + 1) * chan] = (
                        picked[be * quarter : (be + 1) * quarter]
                    )
    pre = None
    for a in range(3):
        rows = second_weight[(9 * a + 3) * chan : 9 * (a + 1) * chan, :]
        term = dot(taps[:, 6 * a * chan : 6 * (a + 1) * chan], rows)
        pre = term if pre is None else pre + term
    delta = cotangent.astype(F32) * gradient_silu(pre)
    delta_ref[...] = delta.T.astype(BF)
    share = 9 * chan
    for ref, half in ((kept_ref, parity[0]), (sent_ref, 1 - parity[0])):
        start = pl.multiple_of(half * share, 128)
        ref[:, :share] = taps[:quarter, pl.ds(start, share)]
        ref[:, share:] = delta[:quarter].astype(BF)


def backward_kernel(
    below, own, delta, pre_ref, kept, got, first_weight, second_weight, volume_ref, grad_ref
):
    chan_in, cells = 64, 128
    chan = pre_ref.shape[1]
    up_first = picker(128, 768, up_first_test)
    up_second = picker(64, 1536, up_second_test)
    spread = dot(delta[...], up_second).astype(BF)
    lanes = spread.shape[1] // 12
    deltas = []
    for h, pairs in enumerate((((1, 0),), ((2, 0), (0, 1)), ((1, 1),))):
        total = None
        for a, i in pairs:
            for be in range(6):
                start = (9 * a + 3 + be) * chan
                term = dot(
                    second_weight[start : start + chan, :],
                    spread[:, (6 * i + be) * lanes : (6 * i + be + 1) * lanes],
                )
                total = term if total is None else total + term
        deltas.append((total * gradient_silu(pre_ref[h])).astype(BF))
    raised = dot(jnp.concatenate(deltas, 0), up_first).astype(BF)
    wide = 2 * cells
    stacks = [
        jnp.concatenate(
            [raised[h * chan : (h + 1) * chan, e * wide : (e + 1) * wide] for e in range(3)], 0
        )
        for h in range(3)
    ]

    def filters(a):
        return [
            jnp.concatenate([first_weight[9 * a + 3 * b + e] for e in range(3)], 1) for b in range(3)
        ]

    totals = {}
    for h, chosen in enumerate(((1, 2), (0, 1, 2), (0,))):
        left = jnp.concatenate(sum([filters(a) for a in chosen], []), 0)
        result = dot(left, stacks[h])
        for place, a in enumerate(chosen):
            p = 2 * h + a - 1
            for b in range(3):
                for j in range(2):
                    r = 2 * j + b - 1
                    if r < 0:
                        continue
                    start = (3 * place + b) * chan_in
                    term = result[start : start + chan_in, j * cells : (j + 1) * cells]
                    totals[p, r] = totals[p, r] + term if (p, r) in totals else term
    for (p, r), total in totals.items():
        volume_ref[p, r] = total.astype(BF)

    def plane(p, r):
        ref, start = (below, (8 + r) * chan_in) if p < 0 else (own, (4 * p + r) * chan_in)
        return ref[start : start + chan_in, :]

    blank = jnp.zeros((chan_in, cells), BF)
    lefts = []
    for a in range(3):
        for b in range(3):
            pieces = []
            for i in range(2):
                for j in range(2):
                    r = 2 * j + b - 1
                    pieces.append(blank if r < 0 else plane(2 * i + a - 1, r))
            lefts.append(jnp.concatenate(pieces, 1))
    grads = dot_rows(jnp.concatenate(lefts, 0), jnp.concatenate(stacks[:2], 1)).astype(BF)
    chunk = 28 * chan_in // grad_ref.shape[0]
    for tap in range(28):
        if tap < 27:
            ab, e = tap // 3, tap % 3
            value = grads[ab * chan_in : (ab + 1) * chan_in, e * chan : (e + 1) * chan]
        else:
            value = jnp.zeros((chan_in, chan), BF)
        at, stop = tap * chan_in, (tap + 1) * chan_in
        while at < stop:
            m, offset = at // chunk, at % chunk
            count = min(stop - at, chunk - offset)
            begin = at - tap * chan_in
            grad_ref[m, offset : offset + count, :] = value[begin : begin + count]
            at += count
    share = 9 * chan
    both = jnp.concatenate([kept[...], got[...]], 0)
    ordered = dot(both[:, share:], picker(256, 256, reorder_test)).astype(BF)
    second = lax.dot_general(
        ordered, both[:, :share], (((0,), (0,)), ((), ())), preferred_element_type=F32
    ).astype(BF)
    second = jnp.concatenate([second, jnp.zeros((second.shape[0], chan), BF)], 1)
    per = 32 // grad_ref.shape[0]
    for piece in range(32):
        o, h = piece // 2, piece % 2
        for lane in range(5):
            start = chunk + (piece % per * 5 + lane) * 16
            grad_ref[piece // per, start : start + 16, :] = second[
                o * 16 : (o + 1) * 16, (5 * h + lane) * chan : (5 * h + lane + 1) * chan
            ]


def exchanged(parts, axis):
    return lax.all_to_all(parts, axis, split_axis=0, concat_axis=0, tiled=True)


def everywhere(value, axis):
    return exchanged(jnp.broadcast_to(value[None], (lax.axis_size(axis),) + value.shape), axis)


def call(kernel, outs, scratch, flops, moved, scalars=0, inputs=0):
    places = [pltpu.SMEM] * scalars + [pltpu.VMEM] * inputs
    return pl.pallas_call(
        kernel,
        out_shape=outs,
        in_specs=[pl.BlockSpec(memory_space=place) for place in places],
        scratch_shapes=scratch,
        compiler_params=pltpu.CompilerParams(vmem_limit_bytes=24 << 20),
        cost_estimate=pl.CostEstimate(flops=flops, bytes_accessed=moved, transcendentals=0),
    )


def shards(input_field, out_cotangent, first_weight, second_weight):
    chan_in, planes, height, length = input_field.shape[1:]
    chan_mid, chan_out = second_weight.shape[1:]
    groups = lax.axis_size("space")
    samples_n = lax.axis_size("sample")
    rows, half, quarter = (height // 2, length // 2, length // 4)
    per_group = chan_out // groups
    own = input_field[0].transpose(1, 2, 0, 3).reshape(-1, length)
    below = shifted(own[height * chan_in :], "space", 1)
    cotangent = out_cotangent[0].reshape(2, chan_out // 2, quarter).transpose(0, 2, 1)
    own = jnp.concatenate([own, cotangent.reshape(2 * quarter, chan_out // 2)], 0)
    above = shifted(own, "space", -1)
    flipped = first_weight.reshape(27 * chan_in, chan_mid).T
    flat_second = second_weight.reshape(27 * chan_mid, chan_out)
    share = 9 * chan_mid
    parity = (lax.axis_index("space") % 2).astype(jnp.int32).reshape(1)
    pre, delta, kept, sent = call(
        forward_kernel,
        (
            jax.ShapeDtypeStruct((3, chan_mid, rows * half), F32),
            jax.ShapeDtypeStruct((chan_out, 2 * quarter), BF),
            jax.ShapeDtypeStruct((quarter, share + chan_out), BF),
            jax.ShapeDtypeStruct((quarter, share + chan_out), BF),
        ),
        [
            pltpu.VMEM((11 * 9 * chan_in, rows * half), BF),
            pltpu.VMEM((2 * quarter, 18 * chan_mid), BF),
        ],
        2_000_000_000,
        6_000_000,
        1,
        5,
    )(parity, below, own, above, flipped, flat_second)
    got = lax.ppermute(sent, "space", [(i, i ^ 1) for i in range(groups)])
    size = 28 * chan_in // samples_n
    pieces = 32 // samples_n * 5
    volume, partial = call(
        backward_kernel,
        (
            jax.ShapeDtypeStruct((planes, height, chan_in, length), BF),
            jax.ShapeDtypeStruct((samples_n, size + pieces * groups, chan_mid), BF),
        ),
        [],
        3_000_000_000,
        6_000_000,
        0,
        8,
    )(below, own, delta, pre, kept, got, first_weight, flat_second)
    input_grad = volume.transpose(2, 0, 1, 3)[None]
    chunk = jnp.sum(exchanged(partial, "sample").astype(F32), 0)
    first_chunk = jnp.broadcast_to(chunk[None, :size], (groups, size, chan_mid))
    second_chunk = chunk[size:].reshape(pieces, groups, chan_mid).transpose(1, 0, 2)
    second_chunk = jnp.pad(second_chunk, ((0, 0), (0, -pieces % 8), (0, 0)))
    both = exchanged(jnp.concatenate([first_chunk, second_chunk], 1).astype(BF), "space")
    first_ext = planes // 2 * rows * half
    first_scale = 1.0 / math.sqrt(samples_n * groups * first_ext)
    second_scale = 1.0 / math.sqrt(samples_n * groups * (planes // 4) * (height // 4) * quarter)
    first_chunk = jnp.sum(both[:, :size].astype(F32), 0) * first_scale
    second_chunk = both[:, size : size + pieces].astype(F32).reshape(groups // 2, 2, pieces, chan_mid)
    second_chunk = (jnp.sum(second_chunk, 0) * second_scale).reshape(2 * pieces, chan_mid)
    second_chunk = jnp.pad(second_chunk, ((0, -2 * pieces % 8), (0, 0)))
    final = everywhere(jnp.concatenate([first_chunk, second_chunk], 0).astype(BF), "sample")
    first_grad = final[:, :size].reshape(28, chan_in, chan_mid)[:27]
    second = final[:, size : size + 2 * pieces].reshape(samples_n, 2, 32 // samples_n, 5, chan_mid)
    second = second.transpose(0, 2, 1, 3, 4).reshape(per_group, 2, 2, 5, chan_mid)
    second = second.transpose(2, 1, 3, 0, 4).reshape(2, 10, per_group, chan_mid)[:, :9]
    second = second.reshape(3, 2, 3, per_group, chan_mid)
    second = jnp.pad(second, ((0, 0), (1, 0), (0, 0), (0, 0), (0, 0)))
    second_grad = second.reshape(27, per_group, chan_mid).transpose(0, 2, 1)
    return input_grad, first_grad, second_grad


def solution(mesh):
    placed = (
        P("sample", None, "space", None, None),
        P("sample", None, "space", None, None),
        P(),
        P(),
    )
    return jax.shard_map(
        shards,
        mesh=mesh,
        in_specs=placed,
        out_specs=(P("sample", None, "space", None, None), P(), P(None, None, "space")),
        check_vma=False,
    )
```

```python
import math

import jax
import jax.numpy as jnp
from jax import lax
from jax.experimental import pallas as pl
from jax.experimental.pallas import tpu as pltpu
from jax.sharding import PartitionSpec as P

BF = jnp.bfloat16
F32 = jnp.float32


def gradient_silu(values):
    logistic = jax.nn.sigmoid(values)
    return logistic * (1.0 + values * (1.0 - logistic))


def dot(left, right):
    return jnp.dot(left, right, preferred_element_type=F32)


def dot_rows(left, right):
    return lax.dot_general(left, right, (((1,), (1,)), ((), ())), preferred_element_type=F32)


def picker(rows, columns, test):
    r = lax.broadcasted_iota(jnp.int32, (rows, columns), 0)
    c = lax.broadcasted_iota(jnp.int32, (rows, columns), 1)
    return jnp.where(test(r, c), 1.0, 0.0).astype(BF)


def down_first_test(r, c):
    return ((r >> 7) == ((c >> 6) & 1)) & ((r & 127) == 2 * (c & 63) + (c >> 7) - 1)


def up_first_test(r, c):
    return ((r >> 6) == ((c >> 7) & 1)) & ((c & 127) == 2 * (r & 63) + (c >> 8) - 1)


def down_second_test(r, c):
    be = r >> 5
    b = jnp.where(be >= 3, 1, 0)
    return (b == (c >> 6)) & ((c & 63) == 2 * (r & 31) + be - 3 * b - 1)


def up_second_test(r, c):
    ibe = c >> 7
    i = jnp.where(ibe >= 6, 1, 0)
    be = ibe - 6 * i
    b = jnp.where(be >= 3, 1, 0)
    return ((r >> 5) == i) & (b == ((c >> 6) & 1)) & ((c & 63) == 2 * (r & 31) + be - 3 * b - 1)


def reorder_test(r, c):
    return ((r >> 4) == (c & 15)) & ((r & 15) == (c >> 4))


def kernel(
    scalars, below, own, above, flipped, first_weight, second_weight, volume_ref, grad_ref, blocks, taps
):
    parity, inside = scalars[0], scalars[1] > 0
    chan_in, cells = 64, 128
    group = 9 * chan_in
    down_first = picker(2 * cells, 3 * 128, down_first_test)
    down_second = picker(192, 128, down_second_test)
    first = 0
    for part, planes, skip in ((below, 3, 4), (own, 4, 0), (above, 4, 0)):

        def row(r):
            lines = [
                part[(4 * p + r + skip) * chan_in : (4 * p + r + skip + 1) * chan_in, :]
                for p in range(planes)
            ]
            return jnp.concatenate(lines, 0)

        for b in range(3):
            if b == 0:
                picked = dot(row(1), down_first[cells:, :])
            else:
                picked = dot(jnp.concatenate([row(b - 1), row(b + 1)], 1), down_first)
            picked = picked.astype(BF)
            for p in range(planes):
                for e in range(3):
                    start = (first + p) * group + (3 * b + e) * chan_in
                    blocks[start : start + chan_in, :] = picked[
                        p * chan_in : (p + 1) * chan_in, e * 128 : (e + 1) * 128
                    ]
        first += planes
    quarter = 32
    lines = 16 * chan_in
    cotangent = jnp.concatenate(
        [
            part[lines + 16 * tile + 8 * half : lines + 16 * tile + 8 * half + 8, :].astype(F32)
            for half in range(2)
            for part in (own, above)
            for tile in range(4)
        ],
        0,
    )
    cotangent = jnp.concatenate([cotangent[:64], cotangent[64:]], 1)
    pres = []
    for h in range(5):
        if h == 3:
            pre = jnp.where(inside, dot(flipped[:, :group], blocks[6 * group : 7 * group, :]), 0.0)
            pre = pre + dot(flipped[:, group:], blocks[7 * group : 9 * group, :])
        else:
            pre = dot(flipped[...], blocks[2 * h * group : (2 * h + 3) * group, :])
        pres.append(pre)
        hidden = (pre * jax.nn.sigmoid(pre)).astype(BF)
        chan = hidden.shape[0]
        picked = dot_rows(down_second, hidden)
        for i in range(2):
            a = h - 2 * i
            if 0 <= a <= 2:
                masked = jnp.where(inside, picked, 0.0) if (i, a) == (1, 0) else picked
                masked = masked.astype(BF)
                for be in range(6):
                    taps[i * quarter : (i + 1) * quarter, (6 * a + be) * chan : (6 * a + be + 1) * chan] = (
                        masked[be * quarter : (be + 1) * quarter]
                    )
    pre = None
    for a in range(3):
        rows = second_weight[(9 * a + 3) * chan : 9 * (a + 1) * chan, :]
        term = dot(taps[:, 6 * a * chan : 6 * (a + 1) * chan], rows)
        pre = term if pre is None else pre + term
    ended = cotangent * gradient_silu(pre)
    delta = jnp.concatenate([ended[:quarter], jnp.where(inside, ended[quarter:], 0.0)], 0).T
    delta = delta.astype(BF)
    up_first = picker(128, 768, up_first_test)
    up_second = picker(64, 1536, up_second_test)
    spread = dot(delta, up_second).astype(BF)
    lanes = spread.shape[1] // 12
    deltas = []
    for h, pairs in enumerate((((1, 0),), ((2, 0), (0, 1)), ((1, 1),))):
        total = None
        for a, i in pairs:
            for be in range(6):
                start = (9 * a + 3 + be) * chan
                term = dot(
                    second_weight[start : start + chan, :],
                    spread[:, (6 * i + be) * lanes : (6 * i + be + 1) * lanes],
                )
                total = term if total is None else total + term
        deltas.append((total * gradient_silu(pres[h + 1])).astype(BF))
    raised = dot(jnp.concatenate(deltas, 0), up_first).astype(BF)
    wide = 2 * cells
    stacks = [
        jnp.concatenate(
            [raised[h * chan : (h + 1) * chan, e * wide : (e + 1) * wide] for e in range(3)], 0
        )
        for h in range(3)
    ]

    def filters(a):
        return [
            jnp.concatenate([first_weight[9 * a + 3 * b + e] for e in range(3)], 1) for b in range(3)
        ]

    totals = {}
    for h, chosen in enumerate(((1, 2), (0, 1, 2), (0,))):
        left = jnp.concatenate(sum([filters(a) for a in chosen], []), 0)
        result = dot(left, stacks[h])
        for place, a in enumerate(chosen):
            p = 2 * h + a - 1
            for b in range(3):
                for j in range(2):
                    r = 2 * j + b - 1
                    if r < 0:
                        continue
                    start = (3 * place + b) * chan_in
                    term = result[start : start + chan_in, j * cells : (j + 1) * cells]
                    totals[p, r] = totals[p, r] + term if (p, r) in totals else term
    for (p, r), total in totals.items():
        volume_ref[p, r] = total.astype(BF)

    def plane(p, r):
        ref, start = (below, (12 + r) * chan_in) if p < 0 else (own, (4 * p + r) * chan_in)
        return ref[start : start + chan_in, :]

    blank = jnp.zeros((chan_in, cells), BF)
    lefts = []
    for a in range(3):
        for b in range(3):
            pieces = []
            for i in range(2):
                for j in range(2):
                    r = 2 * j + b - 1
                    pieces.append(blank if r < 0 else plane(2 * i + a - 1, r))
            lefts.append(jnp.concatenate(pieces, 1))
    grads = dot_rows(jnp.concatenate(lefts, 0), jnp.concatenate(stacks[:2], 1)).astype(BF)
    chunk = 28 * chan_in // grad_ref.shape[0]
    for tap in range(28):
        if tap < 27:
            ab, e = tap // 3, tap % 3
            value = grads[ab * chan_in : (ab + 1) * chan_in, e * chan : (e + 1) * chan]
        else:
            value = jnp.zeros((chan_in, chan), BF)
        at, stop = tap * chan_in, (tap + 1) * chan_in
        while at < stop:
            m, offset = at // chunk, at % chunk
            count = min(stop - at, chunk - offset)
            begin = at - tap * chan_in
            grad_ref[m, offset : offset + count, :] = value[begin : begin + count]
            at += count
    share = 9 * chan
    fields = taps[:, pl.ds(pl.multiple_of(parity * share, 128), share)]
    ordered = dot(ended.astype(BF), picker(256, 256, reorder_test)).astype(BF)
    second = lax.dot_general(
        ordered, fields, (((0,), (0,)), ((), ())), preferred_element_type=F32
    ).astype(BF)
    second = jnp.concatenate([second, jnp.zeros((second.shape[0], chan), BF)], 1)
    per = 32 // grad_ref.shape[0]
    for piece in range(32):
        o, h = piece // 2, piece % 2
        for lane in range(5):
            start = chunk + (piece % per * 5 + lane) * 16
            grad_ref[piece // per, start : start + 16, :] = second[
                o * 16 : (o + 1) * 16, (5 * h + lane) * chan : (5 * h + lane + 1) * chan
            ]


def exchanged(parts, axis):
    return lax.all_to_all(parts, axis, split_axis=0, concat_axis=0, tiled=True)


def everywhere(value, axis):
    return exchanged(jnp.broadcast_to(value[None], (lax.axis_size(axis),) + value.shape), axis)


def shards(input_field, out_cotangent, first_weight, second_weight):
    chan_in, planes, height, length = input_field.shape[1:]
    chan_mid, chan_out = second_weight.shape[1:]
    groups = lax.axis_size("space")
    samples_n = lax.axis_size("sample")
    rows, half, quarter = (height // 2, length // 2, length // 4)
    per_group = chan_out // groups
    own = input_field[0].transpose(1, 2, 0, 3).reshape(-1, length)
    cotangent = out_cotangent[0].reshape(chan_out, quarter).T.reshape(4, 8, 2, 128)
    own = jnp.concatenate([own, cotangent.transpose(0, 2, 1, 3).reshape(64, 128)], 0)
    above = lax.ppermute(own, "space", [(i, (i - 1) % groups) for i in range(groups)])
    below = lax.ppermute(own, "space", [(i, i + 1) for i in range(groups - 1)])
    flipped = first_weight.reshape(27 * chan_in, chan_mid).T
    flat_second = second_weight.reshape(27 * chan_mid, chan_out)
    place = lax.axis_index("space")
    scalars = jnp.where(
        jnp.arange(2) == 0, place % 2, jnp.where(place == groups - 1, 0, 1)
    ).astype(jnp.int32)
    size = 28 * chan_in // samples_n
    pieces = 32 // samples_n * 5
    volume, partial = pl.pallas_call(
        kernel,
        out_shape=(
            jax.ShapeDtypeStruct((planes, height, chan_in, length), BF),
            jax.ShapeDtypeStruct((samples_n, size + pieces * groups, chan_mid), BF),
        ),
        in_specs=[pl.BlockSpec(memory_space=pltpu.SMEM)]
        + [pl.BlockSpec(memory_space=pltpu.VMEM)] * 6,
        scratch_shapes=[
            pltpu.VMEM((11 * 9 * chan_in, rows * half), BF),
            pltpu.VMEM((2 * quarter, 18 * chan_mid), BF),
        ],
        compiler_params=pltpu.CompilerParams(vmem_limit_bytes=24 << 20),
        cost_estimate=pl.CostEstimate(
            flops=5_000_000_000, bytes_accessed=8_000_000, transcendentals=0
        ),
    )(scalars, below, own, above, flipped, first_weight, flat_second)
    input_grad = volume.transpose(2, 0, 1, 3)[None]
    chunk = jnp.sum(exchanged(partial, "sample").astype(F32), 0)
    first_chunk = jnp.broadcast_to(chunk[None, :size], (groups, size, chan_mid))
    second_chunk = chunk[size:].reshape(pieces, groups, chan_mid).transpose(1, 0, 2)
    second_chunk = jnp.pad(second_chunk, ((0, 0), (0, -pieces % 8), (0, 0)))
    both = exchanged(jnp.concatenate([first_chunk, second_chunk], 1).astype(BF), "space")
    first_ext = planes // 2 * rows * half
    first_scale = 1.0 / math.sqrt(samples_n * groups * first_ext)
    second_scale = 1.0 / math.sqrt(samples_n * groups * (planes // 4) * (height // 4) * quarter)
    first_chunk = jnp.sum(both[:, :size].astype(F32), 0) * first_scale
    second_chunk = both[:, size : size + pieces].astype(F32).reshape(groups // 2, 2, pieces, chan_mid)
    second_chunk = (jnp.sum(second_chunk, 0) * second_scale).reshape(2 * pieces, chan_mid)
    second_chunk = jnp.pad(second_chunk, ((0, -2 * pieces % 8), (0, 0)))
    final = everywhere(jnp.concatenate([first_chunk, second_chunk], 0).astype(BF), "sample")
    first_grad = final[:, :size].reshape(28, chan_in, chan_mid)[:27]
    second = final[:, size : size + 2 * pieces].reshape(samples_n, 2, 32 // samples_n, 5, chan_mid)
    second = second.transpose(0, 2, 1, 3, 4).reshape(per_group, 2, 2, 5, chan_mid)
    second = second.transpose(2, 1, 3, 0, 4).reshape(2, 10, per_group, chan_mid)[:, :9]
    second = second.reshape(3, 2, 3, per_group, chan_mid)
    second = jnp.pad(second, ((0, 0), (1, 0), (0, 0), (0, 0), (0, 0)))
    second_grad = second.reshape(27, per_group, chan_mid).transpose(0, 2, 1)
    return input_grad, first_grad, second_grad


def solution(mesh):
    placed = (
        P("sample", None, "space", None, None),
        P("sample", None, "space", None, None),
        P(),
        P(),
    )
    return jax.shard_map(
        shards,
        mesh=mesh,
        in_specs=placed,
        out_specs=(P("sample", None, "space", None, None), P(), P(None, None, "space")),
        check_vma=False,
    )
```

```python
import math

import jax
import jax.numpy as jnp
from jax import lax
from jax.experimental import pallas as pl
from jax.experimental.pallas import tpu as pltpu
from jax.sharding import PartitionSpec as P

BF = jnp.bfloat16
F32 = jnp.float32


def gradient_silu(values):
    logistic = jax.nn.sigmoid(values)
    return logistic * (1.0 + values * (1.0 - logistic))


def dot(left, right):
    return jnp.dot(left, right, preferred_element_type=F32)


def dot_rows(left, right):
    return lax.dot_general(left, right, (((1,), (1,)), ((), ())), preferred_element_type=F32)


def picker(rows, columns, test):
    r = lax.broadcasted_iota(jnp.int32, (rows, columns), 0)
    c = lax.broadcasted_iota(jnp.int32, (rows, columns), 1)
    return jnp.where(test(r, c), 1.0, 0.0).astype(BF)


def down_first_test(r, c):
    return ((r >> 7) == ((c >> 6) & 1)) & ((r & 127) == 2 * (c & 63) + (c >> 7) - 1)


def up_first_test(r, c):
    return ((r >> 6) == ((c >> 7) & 1)) & ((c & 127) == 2 * (r & 63) + (c >> 8) - 1)


def down_second_test(r, c):
    be = r >> 5
    b = jnp.where(be >= 3, 1, 0)
    return (b == (c >> 6)) & ((c & 63) == 2 * (r & 31) + be - 3 * b - 1)


def up_second_test(r, c):
    ibe = c >> 7
    i = jnp.where(ibe >= 6, 1, 0)
    be = ibe - 6 * i
    b = jnp.where(be >= 3, 1, 0)
    return ((r >> 5) == i) & (b == ((c >> 6) & 1)) & ((c & 63) == 2 * (r & 31) + be - 3 * b - 1)


def reorder_test(r, c):
    return ((r >> 4) == (c & 15)) & ((r & 15) == (c >> 4))


def main_kernel(
    scalars, below, own, above, flipped, second_hbm,
    stacks_ref, kept_ref, sent_ref, second_ref,
    blocks, taps, grads, second_weight, sems,
):
    copies = []
    for a in range(3):
        size = second_weight.shape[1]
        start = 3 * a * size // 2 + size // 2
        copies.append(
            pltpu.make_async_copy(second_hbm.at[start : start + size], second_weight.at[a], sems.at[a])
        )
        copies[a].start()
    parity, inside = scalars[0], scalars[1] > 0
    chan_in, cells = 64, 128
    group = 9 * chan_in
    down_first = picker(2 * cells, 3 * 128, down_first_test)
    down_second = picker(192, 128, down_second_test)
    first = 0
    for part, planes, skip in ((below, 3, 4), (own, 4, 0), (above, 4, 0)):

        def row(r):
            lines = [
                part[(4 * p + r + skip) * chan_in : (4 * p + r + skip + 1) * chan_in, :]
                for p in range(planes)
            ]
            return jnp.concatenate(lines, 0)

        for b in range(3):
            if b == 0:
                picked = dot(row(1), down_first[cells:, :])
            else:
                picked = dot(jnp.concatenate([row(b - 1), row(b + 1)], 1), down_first)
            picked = picked.astype(BF)
            for p in range(planes):
                for e in range(3):
                    start = (first + p) * group + (3 * b + e) * chan_in
                    blocks[start : start + chan_in, :] = picked[
                        p * chan_in : (p + 1) * chan_in, e * 128 : (e + 1) * 128
                    ]
        first += planes
    quarter = 32
    lines = 16 * chan_in
    cotangent = jnp.concatenate(
        [
            part[lines + 16 * tile + 8 * half : lines + 16 * tile + 8 * half + 8, :].astype(F32)
            for half in range(2)
            for part in (own, above)
            for tile in range(4)
        ],
        0,
    )
    cotangent = jnp.concatenate([cotangent[:64], cotangent[64:]], 1)
    pres = []
    for h in range(5):
        if h == 3:
            pre = jnp.where(inside, dot(flipped[:, :group], blocks[6 * group : 7 * group, :]), 0.0)
            pre = pre + dot(flipped[:, group:], blocks[7 * group : 9 * group, :])
        else:
            pre = dot(flipped[...], blocks[2 * h * group : (2 * h + 3) * group, :])
        pres.append(pre)
        hidden = (pre * jax.nn.sigmoid(pre)).astype(BF)
        chan = hidden.shape[0]
        picked = dot_rows(down_second, hidden)
        for i in range(2):
            a = h - 2 * i
            if 0 <= a <= 2:
                masked = jnp.where(inside, picked, 0.0) if (i, a) == (1, 0) else picked
                masked = masked.astype(BF)
                for be in range(6):
                    taps[i * quarter : (i + 1) * quarter, (6 * a + be) * chan : (6 * a + be + 1) * chan] = (
                        masked[be * quarter : (be + 1) * quarter]
                    )
    pre = None
    for a in range(3):
        copies[a].wait()
        term = dot(taps[:, 6 * a * chan : 6 * (a + 1) * chan], second_weight[a])
        pre = term if pre is None else pre + term
    ended = cotangent * gradient_silu(pre)
    delta = jnp.concatenate([ended[:quarter], jnp.where(inside, ended[quarter:], 0.0)], 0).T
    delta = delta.astype(BF)
    up_first = picker(128, 768, up_first_test)
    up_second = picker(64, 1536, up_second_test)
    spread = dot(delta, up_second).astype(BF)
    lanes = spread.shape[1] // 12
    deltas = []
    for h, pairs in enumerate((((1, 0),), ((2, 0), (0, 1)), ((1, 1),))):
        total = None
        for a, i in pairs:
            for be in range(6):
                term = dot(
                    second_weight[a, be * chan : (be + 1) * chan, :],
                    spread[:, (6 * i + be) * lanes : (6 * i + be + 1) * lanes],
                )
                total = term if total is None else total + term
        deltas.append((total * gradient_silu(pres[h + 1])).astype(BF))
    raised = dot(jnp.concatenate(deltas, 0), up_first).astype(BF)
    wide = 2 * cells
    stacks = [
        jnp.concatenate(
            [raised[h * chan : (h + 1) * chan, e * wide : (e + 1) * wide] for e in range(3)], 0
        )
        for h in range(3)
    ]

    for h in range(3):
        stacks_ref[h] = stacks[h]

    def plane(p, r):
        ref, start = (below, (12 + r) * chan_in) if p < 0 else (own, (4 * p + r) * chan_in)
        return ref[start : start + chan_in, :]

    blank = jnp.zeros((chan_in, cells), BF)
    lefts = []
    for a in range(3):
        for b in range(3):
            pieces = []
            for i in range(2):
                for j in range(2):
                    r = 2 * j + b - 1
                    pieces.append(blank if r < 0 else plane(2 * i + a - 1, r))
            lefts.append(jnp.concatenate(pieces, 1))
    result = dot_rows(jnp.concatenate(lefts, 0), jnp.concatenate(stacks[:2], 1))
    for ab in range(9):
        for e in range(3):
            start = (3 * ab + e) * chan_in
            grads[start : start + chan_in, :] = result[
                ab * chan_in : (ab + 1) * chan_in, e * chan : (e + 1) * chan
            ]
    grads[27 * chan_in :, :] = jnp.zeros((chan_in, chan), F32)
    samples_n, size = kept_ref.shape[:2]
    for m in range(samples_n):
        lower = grads[2 * m * size : (2 * m + 1) * size, :]
        upper = grads[(2 * m + 1) * size : (2 * m + 2) * size, :]
        kept_ref[m] = jnp.where(parity == 0, lower, upper).astype(BF)
        sent_ref[m] = jnp.where(parity == 0, upper, lower).astype(BF)
    share = 9 * chan
    fields = taps[:, pl.ds(pl.multiple_of(parity * share, 128), share)]
    ordered = dot(ended.astype(BF), picker(256, 256, reorder_test)).astype(BF)
    second = lax.dot_general(
        ordered, fields, (((0,), (0,)), ((), ())), preferred_element_type=F32
    ).astype(BF)
    per = 32 // samples_n
    for piece in range(32):
        m, at = piece // per, piece % per * 72
        first = piece // 2 * 16
        for lane in range(4, 9) if piece % 2 else range(5):
            begin = first + 8 if lane == 4 and piece % 2 else first
            count = 8 if lane == 4 else 16
            second_ref[m, at : at + count, :] = second[
                begin : begin + count, lane * chan : (lane + 1) * chan
            ]
            at += count


def volume_kernel(stacks, first_weight, volume_ref):
    chan_in, cells = volume_ref.shape[2:]

    def filters(a):
        return [
            jnp.concatenate([first_weight[9 * a + 3 * b + e] for e in range(3)], 1) for b in range(3)
        ]

    totals = {}
    for h, chosen in enumerate(((1, 2), (0, 1, 2), (0,))):
        left = jnp.concatenate(sum([filters(a) for a in chosen], []), 0)
        result = dot(left, stacks[h])
        for place, a in enumerate(chosen):
            p = 2 * h + a - 1
            for b in range(3):
                for j in range(2):
                    r = 2 * j + b - 1
                    if r < 0:
                        continue
                    start = (3 * place + b) * chan_in
                    term = result[start : start + chan_in, j * cells : (j + 1) * cells]
                    totals[p, r] = totals[p, r] + term if (p, r) in totals else term
    for (p, r), total in totals.items():
        volume_ref[p, r] = total.astype(BF)


def pack_kernel(second, kept, got, payload_ref):
    rows = second.shape[1]
    for m in range(second.shape[0]):
        payload_ref[m, :rows, :] = second[m]
        payload_ref[m, rows:, :] = (kept[m].astype(F32) + got[m].astype(F32)).astype(BF)


def exchanged(parts, axis):
    return lax.all_to_all(parts, axis, split_axis=0, concat_axis=0, tiled=True)


def everywhere(value, axis):
    return exchanged(jnp.broadcast_to(value[None], (lax.axis_size(axis),) + value.shape), axis)


def shards(input_field, out_cotangent, first_weight, second_weight):
    chan_in, planes, height, length = input_field.shape[1:]
    chan_mid, chan_out = second_weight.shape[1:]
    groups = lax.axis_size("space")
    samples_n = lax.axis_size("sample")
    rows, half, quarter = (height // 2, length // 2, length // 4)
    per_group = chan_out // groups
    own = input_field[0].transpose(1, 2, 0, 3).reshape(-1, length)
    cotangent = out_cotangent[0].reshape(chan_out, quarter).T.reshape(4, 8, 2, 128)
    own = jnp.concatenate([own, cotangent.transpose(0, 2, 1, 3).reshape(64, 128)], 0)
    above = lax.ppermute(own, "space", [(i, (i - 1) % groups) for i in range(groups)])
    below = lax.ppermute(own, "space", [(i, i + 1) for i in range(groups - 1)])
    flipped = first_weight.reshape(27 * chan_in, chan_mid).T
    flat_second = second_weight.reshape(27 * chan_mid, chan_out)
    place = lax.axis_index("space")
    scalars = jnp.where(
        jnp.arange(2) == 0, place % 2, jnp.where(place == groups - 1, 0, 1)
    ).astype(jnp.int32)
    size = 14 * chan_in // samples_n
    per = 32 // samples_n
    vmem = pl.BlockSpec(memory_space=pltpu.VMEM)
    stacks, kept, sent, second = pl.pallas_call(
        main_kernel,
        out_shape=(
            jax.ShapeDtypeStruct((3, 3 * chan_mid, 2 * length), BF),
            jax.ShapeDtypeStruct((samples_n, size, chan_mid), BF),
            jax.ShapeDtypeStruct((samples_n, size, chan_mid), BF),
            jax.ShapeDtypeStruct((samples_n, per * 72, chan_mid), BF),
        ),
        in_specs=[pl.BlockSpec(memory_space=pltpu.SMEM)]
        + [vmem] * 4
        + [pl.BlockSpec(memory_space=pl.ANY)],
        scratch_shapes=[
            pltpu.VMEM((11 * 9 * chan_in, rows * half), BF),
            pltpu.VMEM((2 * quarter, 18 * chan_mid), BF),
            pltpu.VMEM((28 * chan_in, chan_mid), F32),
            pltpu.VMEM((3, 6 * chan_mid, chan_out), BF),
            pltpu.SemaphoreType.DMA((3,)),
        ],
        compiler_params=pltpu.CompilerParams(vmem_limit_bytes=24 << 20),
        cost_estimate=pl.CostEstimate(
            flops=4_000_000_000, bytes_accessed=8_000_000, transcendentals=0
        ),
    )(scalars, below, own, above, flipped, flat_second)
    got = lax.ppermute(sent, "space", [(i, i ^ 1) for i in range(groups)])
    payload = pl.pallas_call(
        pack_kernel,
        out_shape=jax.ShapeDtypeStruct((samples_n, per * 72 + size, chan_mid), BF),
        cost_estimate=pl.CostEstimate(flops=1_000_000, bytes_accessed=2_000_000, transcendentals=0),
    )(second, kept, got)
    volume = pl.pallas_call(
        volume_kernel,
        out_shape=jax.ShapeDtypeStruct((planes, height, chan_in, length), BF),
        compiler_params=pltpu.CompilerParams(vmem_limit_bytes=24 << 20),
        cost_estimate=pl.CostEstimate(
            flops=1_000_000_000, bytes_accessed=2_000_000, transcendentals=0
        ),
    )(stacks, first_weight)
    input_grad = volume.transpose(2, 0, 1, 3)[None]
    chunk = jnp.sum(exchanged(payload, "sample").astype(F32), 0)
    first_chunk = jnp.broadcast_to(chunk[None, per * 72 :], (groups, size, chan_mid))
    second_chunk = chunk[: per * 72].reshape(per, 72, chan_mid)
    odd = (lax.axis_index("sample") * per + jnp.arange(per)) % 2 == 1
    second_chunk = jnp.where(
        odd[:, None, None],
        jnp.pad(second_chunk, ((0, 0), (8, 0), (0, 0))),
        jnp.pad(second_chunk, ((0, 0), (0, 8), (0, 0))),
    )
    pieces = 5 * per
    second_chunk = second_chunk.reshape(pieces, groups, chan_mid).transpose(1, 0, 2)
    second_chunk = jnp.pad(second_chunk, ((0, 0), (0, -(size + pieces) % 8), (0, 0)))
    both = exchanged(jnp.concatenate([first_chunk, second_chunk], 1).astype(BF), "space")
    both = jnp.sum(both.astype(F32).reshape(groups // 2, 2, -1, chan_mid), 0)
    first_ext = planes // 2 * rows * half
    first_scale = 1.0 / math.sqrt(samples_n * groups * first_ext)
    second_scale = 1.0 / math.sqrt(samples_n * groups * (planes // 4) * (height // 4) * quarter)
    first_chunk = both[:, :size].reshape(2 * size, chan_mid) * first_scale
    second_chunk = both[:, size : size + pieces].reshape(2 * pieces, chan_mid) * second_scale
    both = jnp.concatenate([first_chunk, second_chunk], 0)
    both = jnp.pad(both, ((0, -both.shape[0] % 8), (0, 0)))
    final = everywhere(both.astype(BF), "sample")
    first_grad = final[:, : 2 * size].reshape(28, chan_in, chan_mid)[:27]
    second = final[:, 2 * size : 2 * size + 2 * pieces].reshape(samples_n, 2, per, 5, chan_mid)
    second = second.transpose(0, 2, 1, 3, 4).reshape(per_group, 2, 2, 5, chan_mid)
    second = second.transpose(2, 1, 3, 0, 4)
    shared = second[:, 0, 4:] + second[:, 1, :1]
    second = jnp.concatenate([second[:, 0, :4], shared, second[:, 1, 1:]], 1)
    second = second.reshape(3, 2, 3, per_group, chan_mid)
    second = jnp.pad(second, ((0, 0), (1, 0), (0, 0), (0, 0), (0, 0)))
    second_grad = second.reshape(27, per_group, chan_mid).transpose(0, 2, 1)
    return input_grad, first_grad, second_grad


def solution(mesh):
    placed = (
        P("sample", None, "space", None, None),
        P("sample", None, "space", None, None),
        P(),
        P(),
    )
    return jax.shard_map(
        shards,
        mesh=mesh,
        in_specs=placed,
        out_specs=(P("sample", None, "space", None, None), P(), P(None, None, "space")),
        check_vma=False,
    )
```

```python
import math

import jax
import jax.numpy as jnp
from jax import lax
from jax.experimental import pallas as pl
from jax.experimental.pallas import tpu as pltpu
from jax.sharding import PartitionSpec as P

BF = jnp.bfloat16
F32 = jnp.float32


def gradient_silu(values):
    logistic = jax.nn.sigmoid(values)
    return logistic * (1.0 + values * (1.0 - logistic))


def dot(left, right):
    return jnp.dot(left, right, preferred_element_type=F32)


def dot_rows(left, right):
    return lax.dot_general(left, right, (((1,), (1,)), ((), ())), preferred_element_type=F32)


def picker(rows, columns, test):
    r = lax.broadcasted_iota(jnp.int32, (rows, columns), 0)
    c = lax.broadcasted_iota(jnp.int32, (rows, columns), 1)
    return jnp.where(test(r, c), 1.0, 0.0).astype(BF)


def down_first_test(r, c):
    return ((r >> 7) == ((c >> 6) & 1)) & ((r & 127) == 2 * (c & 63) + (c >> 7) - 1)


def up_first_test(r, c):
    return ((r >> 6) == ((c >> 7) & 1)) & ((c & 127) == 2 * (r & 63) + (c >> 8) - 1)


def down_second_test(r, c):
    be = r >> 5
    b = jnp.where(be >= 3, 1, 0)
    return (b == (c >> 6)) & ((c & 63) == 2 * (r & 31) + be - 3 * b - 1)


def up_second_test(r, c):
    ibe = c >> 7
    i = jnp.where(ibe >= 6, 1, 0)
    be = ibe - 6 * i
    b = jnp.where(be >= 3, 1, 0)
    return ((r >> 5) == i) & (b == ((c >> 6) & 1)) & ((c & 63) == 2 * (r & 31) + be - 3 * b - 1)


def reorder_test(r, c):
    return ((r >> 4) == (c & 15)) & ((r & 15) == (c >> 4))


def main_kernel(
    scalars, below, own, above, flipped, second_weight,
    stacks_ref, kept_ref, sent_ref, fields_ref, ordered_ref,
    blocks, taps, grads,
):
    parity, inside = scalars[0], scalars[1] > 0
    chan_in, cells = 64, 128
    group = 9 * chan_in
    down_first = picker(2 * cells, 3 * 128, down_first_test)
    down_second = picker(192, 128, down_second_test)
    first = 0
    for part, planes, skip in ((below, 3, 4), (own, 4, 0), (above, 4, 0)):

        def row(r):
            lines = [
                part[(4 * p + r + skip) * chan_in : (4 * p + r + skip + 1) * chan_in, :]
                for p in range(planes)
            ]
            return jnp.concatenate(lines, 0)

        for b in range(3):
            if b == 0:
                picked = dot(row(1), down_first[cells:, :])
            else:
                picked = dot(jnp.concatenate([row(b - 1), row(b + 1)], 1), down_first)
            picked = picked.astype(BF)
            for p in range(planes):
                for e in range(3):
                    start = (first + p) * group + (3 * b + e) * chan_in
                    blocks[start : start + chan_in, :] = picked[
                        p * chan_in : (p + 1) * chan_in, e * 128 : (e + 1) * 128
                    ]
        first += planes
    quarter = 32
    lines = 16 * chan_in
    cotangent = jnp.concatenate(
        [
            part[lines + 16 * tile + 8 * half : lines + 16 * tile + 8 * half + 8, :].astype(F32)
            for half in range(2)
            for part in (own, above)
            for tile in range(4)
        ],
        0,
    )
    cotangent = jnp.concatenate([cotangent[:64], cotangent[64:]], 1)
    pres = []
    for h in range(5):
        if h == 3:
            pre = jnp.where(inside, dot(flipped[:, :group], blocks[6 * group : 7 * group, :]), 0.0)
            pre = pre + dot(flipped[:, group:], blocks[7 * group : 9 * group, :])
        else:
            pre = dot(flipped[...], blocks[2 * h * group : (2 * h + 3) * group, :])
        pres.append(pre)
        hidden = (pre * jax.nn.sigmoid(pre)).astype(BF)
        chan = hidden.shape[0]
        picked = dot_rows(down_second, hidden)
        for i in range(2):
            a = h - 2 * i
            if 0 <= a <= 2:
                masked = jnp.where(inside, picked, 0.0) if (i, a) == (1, 0) else picked
                masked = masked.astype(BF)
                for be in range(6):
                    taps[i * quarter : (i + 1) * quarter, (6 * a + be) * chan : (6 * a + be + 1) * chan] = (
                        masked[be * quarter : (be + 1) * quarter]
                    )
    pre = None
    for a in range(3):
        rows = second_weight[(9 * a + 3) * chan : 9 * (a + 1) * chan, :]
        term = dot(taps[:, 6 * a * chan : 6 * (a + 1) * chan], rows)
        pre = term if pre is None else pre + term
    ended = cotangent * gradient_silu(pre)
    delta = jnp.concatenate([ended[:quarter], jnp.where(inside, ended[quarter:], 0.0)], 0).T
    delta = delta.astype(BF)
    up_first = picker(128, 768, up_first_test)
    up_second = picker(64, 1536, up_second_test)
    spread = dot(delta, up_second).astype(BF)
    lanes = spread.shape[1] // 12
    deltas = []
    for h, pairs in enumerate((((1, 0),), ((2, 0), (0, 1)), ((1, 1),))):
        total = None
        for a, i in pairs:
            for be in range(6):
                start = (9 * a + 3 + be) * chan
                term = dot(
                    second_weight[start : start + chan, :],
                    spread[:, (6 * i + be) * lanes : (6 * i + be + 1) * lanes],
                )
                total = term if total is None else total + term
        deltas.append((total * gradient_silu(pres[h + 1])).astype(BF))
    raised = dot(jnp.concatenate(deltas, 0), up_first).astype(BF)
    wide = 2 * cells
    stacks = [
        jnp.concatenate(
            [raised[h * chan : (h + 1) * chan, e * wide : (e + 1) * wide] for e in range(3)], 0
        )
        for h in range(3)
    ]

    for h in range(3):
        stacks_ref[h] = stacks[h]

    def plane(p, r):
        ref, start = (below, (12 + r) * chan_in) if p < 0 else (own, (4 * p + r) * chan_in)
        return ref[start : start + chan_in, :]

    blank = jnp.zeros((chan_in, cells), BF)
    lefts = []
    for a in range(3):
        for b in range(3):
            pieces = []
            for i in range(2):
                for j in range(2):
                    r = 2 * j + b - 1
                    pieces.append(blank if r < 0 else plane(2 * i + a - 1, r))
            lefts.append(jnp.concatenate(pieces, 1))
    result = dot_rows(jnp.concatenate(lefts, 0), jnp.concatenate(stacks[:2], 1))
    for ab in range(9):
        for e in range(3):
            start = (3 * ab + e) * chan_in
            grads[start : start + chan_in, :] = result[
                ab * chan_in : (ab + 1) * chan_in, e * chan : (e + 1) * chan
            ]
    grads[27 * chan_in :, :] = jnp.zeros((chan_in, chan), F32)
    samples_n, size = kept_ref.shape[:2]
    for m in range(samples_n):
        lower = grads[2 * m * size : (2 * m + 1) * size, :]
        upper = grads[(2 * m + 1) * size : (2 * m + 2) * size, :]
        kept_ref[m] = jnp.where(parity == 0, lower, upper).astype(BF)
        sent_ref[m] = jnp.where(parity == 0, upper, lower).astype(BF)
    share = 9 * chan
    fields_ref[...] = taps[:, pl.ds(pl.multiple_of(parity * share, 128), share)]
    ordered_ref[...] = dot(ended.astype(BF), picker(256, 256, reorder_test)).astype(BF)


def middle_kernel(stacks, first_weight, fields, ordered, volume_ref, second_ref):
    chan_in, cells = volume_ref.shape[2:]
    chan = fields.shape[1] // 9
    second = lax.dot_general(
        ordered[...], fields[...], (((0,), (0,)), ((), ())), preferred_element_type=F32
    ).astype(BF)
    samples_n = second_ref.shape[0]
    per = 32 // samples_n
    for piece in range(32):
        m, at = piece // per, piece % per * 72
        first = piece // 2 * 16
        for lane in range(4, 9) if piece % 2 else range(5):
            begin = first + 8 if lane == 4 and piece % 2 else first
            count = 8 if lane == 4 else 16
            second_ref[m, at : at + count, :] = second[
                begin : begin + count, lane * chan : (lane + 1) * chan
            ]
            at += count

    def filters(a):
        return [
            jnp.concatenate([first_weight[9 * a + 3 * b + e] for e in range(3)], 1) for b in range(3)
        ]

    totals = {}
    for h, chosen in enumerate(((1, 2), (0, 1, 2), (0,))):
        left = jnp.concatenate(sum([filters(a) for a in chosen], []), 0)
        result = dot(left, stacks[h])
        for place, a in enumerate(chosen):
            p = 2 * h + a - 1
            for b in range(3):
                for j in range(2):
                    r = 2 * j + b - 1
                    if r < 0:
                        continue
                    start = (3 * place + b) * chan_in
                    term = result[start : start + chan_in, j * cells : (j + 1) * cells]
                    totals[p, r] = totals[p, r] + term if (p, r) in totals else term
    for (p, r), total in totals.items():
        volume_ref[p, r] = total.astype(BF)


def pack_kernel(second, kept, got, payload_ref):
    rows = second.shape[1]
    for m in range(second.shape[0]):
        payload_ref[m, :rows, :] = second[m]
        payload_ref[m, rows:, :] = (kept[m].astype(F32) + got[m].astype(F32)).astype(BF)


def exchanged(parts, axis):
    return lax.all_to_all(parts, axis, split_axis=0, concat_axis=0, tiled=True)


def everywhere(value, axis):
    return exchanged(jnp.broadcast_to(value[None], (lax.axis_size(axis),) + value.shape), axis)


def shards(input_field, out_cotangent, first_weight, second_weight):
    chan_in, planes, height, length = input_field.shape[1:]
    chan_mid, chan_out = second_weight.shape[1:]
    groups = lax.axis_size("space")
    samples_n = lax.axis_size("sample")
    rows, half, quarter = (height // 2, length // 2, length // 4)
    per_group = chan_out // groups
    own = input_field[0].transpose(1, 2, 0, 3).reshape(-1, length)
    cotangent = out_cotangent[0].reshape(chan_out, quarter).T.reshape(4, 8, 2, 128)
    own = jnp.concatenate([own, cotangent.transpose(0, 2, 1, 3).reshape(64, 128)], 0)
    above = lax.ppermute(own, "space", [(i, (i - 1) % groups) for i in range(groups)])
    below = lax.ppermute(own, "space", [(i, i + 1) for i in range(groups - 1)])
    flipped = first_weight.reshape(27 * chan_in, chan_mid).T
    flat_second = second_weight.reshape(27 * chan_mid, chan_out)
    place = lax.axis_index("space")
    scalars = jnp.where(
        jnp.arange(2) == 0, place % 2, jnp.where(place == groups - 1, 0, 1)
    ).astype(jnp.int32)
    size = 14 * chan_in // samples_n
    per = 32 // samples_n
    vmem = pl.BlockSpec(memory_space=pltpu.VMEM)
    stacks, kept, sent, fields, ordered = pl.pallas_call(
        main_kernel,
        out_shape=(
            jax.ShapeDtypeStruct((3, 3 * chan_mid, 2 * length), BF),
            jax.ShapeDtypeStruct((samples_n, size, chan_mid), BF),
            jax.ShapeDtypeStruct((samples_n, size, chan_mid), BF),
            jax.ShapeDtypeStruct((2 * quarter, 9 * chan_mid), BF),
            jax.ShapeDtypeStruct((2 * quarter, chan_out), BF),
        ),
        in_specs=[pl.BlockSpec(memory_space=pltpu.SMEM)]
        + [vmem] * 5,
        scratch_shapes=[
            pltpu.VMEM((11 * 9 * chan_in, rows * half), BF),
            pltpu.VMEM((2 * quarter, 18 * chan_mid), BF),
            pltpu.VMEM((28 * chan_in, chan_mid), F32),
        ],
        compiler_params=pltpu.CompilerParams(vmem_limit_bytes=16 << 20),
        cost_estimate=pl.CostEstimate(
            flops=4_000_000_000, bytes_accessed=8_000_000, transcendentals=0
        ),
    )(scalars, below, own, above, flipped, flat_second)
    got = lax.ppermute(sent, "space", [(i, i ^ 1) for i in range(groups)])
    volume, second = pl.pallas_call(
        middle_kernel,
        out_shape=(
            jax.ShapeDtypeStruct((planes, height, chan_in, length), BF),
            jax.ShapeDtypeStruct((samples_n, per * 72, chan_mid), BF),
        ),
        compiler_params=pltpu.CompilerParams(vmem_limit_bytes=8 << 20),
        cost_estimate=pl.CostEstimate(
            flops=1_000_000_000, bytes_accessed=2_000_000, transcendentals=0
        ),
    )(stacks, first_weight, fields, ordered)
    payload = pl.pallas_call(
        pack_kernel,
        out_shape=jax.ShapeDtypeStruct((samples_n, per * 72 + size, chan_mid), BF),
        compiler_params=pltpu.CompilerParams(vmem_limit_bytes=8 << 20),
        cost_estimate=pl.CostEstimate(flops=1_000_000, bytes_accessed=2_000_000, transcendentals=0),
    )(second, kept, got)
    input_grad = volume.transpose(2, 0, 1, 3)[None]
    chunk = jnp.sum(exchanged(payload, "sample").astype(F32), 0)
    first_chunk = jnp.broadcast_to(chunk[None, per * 72 :], (groups, size, chan_mid))
    second_chunk = chunk[: per * 72].reshape(per, 72, chan_mid)
    odd = (lax.axis_index("sample") * per + jnp.arange(per)) % 2 == 1
    second_chunk = jnp.where(
        odd[:, None, None],
        jnp.pad(second_chunk, ((0, 0), (8, 0), (0, 0))),
        jnp.pad(second_chunk, ((0, 0), (0, 8), (0, 0))),
    )
    pieces = 5 * per
    second_chunk = second_chunk.reshape(pieces, groups, chan_mid).transpose(1, 0, 2)
    second_chunk = jnp.pad(second_chunk, ((0, 0), (0, -(size + pieces) % 8), (0, 0)))
    both = exchanged(jnp.concatenate([first_chunk, second_chunk], 1).astype(BF), "space")
    both = jnp.sum(both.astype(F32).reshape(groups // 2, 2, -1, chan_mid), 0)
    first_ext = planes // 2 * rows * half
    first_scale = 1.0 / math.sqrt(samples_n * groups * first_ext)
    second_scale = 1.0 / math.sqrt(samples_n * groups * (planes // 4) * (height // 4) * quarter)
    first_chunk = both[:, :size].reshape(2 * size, chan_mid) * first_scale
    second_chunk = both[:, size : size + pieces].reshape(2 * pieces, chan_mid) * second_scale
    both = jnp.concatenate([first_chunk, second_chunk], 0)
    both = jnp.pad(both, ((0, -both.shape[0] % 8), (0, 0)))
    final = everywhere(both.astype(BF), "sample")
    first_grad = final[:, : 2 * size].reshape(28, chan_in, chan_mid)[:27]
    second = final[:, 2 * size : 2 * size + 2 * pieces].reshape(samples_n, 2, per, 5, chan_mid)
    second = second.transpose(0, 2, 1, 3, 4).reshape(per_group, 2, 2, 5, chan_mid)
    second = second.transpose(2, 1, 3, 0, 4)
    shared = second[:, 0, 4:] + second[:, 1, :1]
    second = jnp.concatenate([second[:, 0, :4], shared, second[:, 1, 1:]], 1)
    second = second.reshape(3, 2, 3, per_group, chan_mid)
    second = jnp.pad(second, ((0, 0), (1, 0), (0, 0), (0, 0), (0, 0)))
    second_grad = second.reshape(27, per_group, chan_mid).transpose(0, 2, 1)
    return input_grad, first_grad, second_grad


def solution(mesh):
    placed = (
        P("sample", None, "space", None, None),
        P("sample", None, "space", None, None),
        P(),
        P(),
    )
    return jax.shard_map(
        shards,
        mesh=mesh,
        in_specs=placed,
        out_specs=(P("sample", None, "space", None, None), P(), P(None, None, "space")),
        check_vma=False,
    )
```

```python
import math

import jax
import jax.numpy as jnp
from jax import lax
from jax.experimental import pallas as pl
from jax.experimental.pallas import tpu as pltpu
from jax.sharding import PartitionSpec as P

BF = jnp.bfloat16
F32 = jnp.float32


def gradient_silu(values):
    logistic = jax.nn.sigmoid(values)
    return logistic * (1.0 + values * (1.0 - logistic))


def dot(left, right):
    return jnp.dot(left, right, preferred_element_type=F32)


def dot_rows(left, right):
    return lax.dot_general(left, right, (((1,), (1,)), ((), ())), preferred_element_type=F32)


def picker(rows, columns, test):
    r = lax.broadcasted_iota(jnp.int32, (rows, columns), 0)
    c = lax.broadcasted_iota(jnp.int32, (rows, columns), 1)
    return jnp.where(test(r, c), 1.0, 0.0).astype(BF)


def down_first_test(r, c):
    return ((r >> 7) == ((c >> 6) & 1)) & ((r & 127) == 2 * (c & 63) + (c >> 7) - 1)


def up_first_test(r, c):
    return ((r >> 6) == ((c >> 7) & 1)) & ((c & 127) == 2 * (r & 63) + (c >> 8) - 1)


def down_second_test(r, c):
    be = r >> 5
    b = jnp.where(be >= 3, 1, 0)
    return (b == (c >> 6)) & ((c & 63) == 2 * (r & 31) + be - 3 * b - 1)


def up_second_test(r, c):
    ibe = c >> 7
    i = jnp.where(ibe >= 6, 1, 0)
    be = ibe - 6 * i
    b = jnp.where(be >= 3, 1, 0)
    return ((r >> 5) == i) & (b == ((c >> 6) & 1)) & ((c & 63) == 2 * (r & 31) + be - 3 * b - 1)


def reorder_test(r, c):
    return ((r >> 4) == (c & 15)) & ((r & 15) == (c >> 4))


def forward_kernel(
    scalars, below, own, above, flipped, second_weight,
    pre_ref, delta_ref, kept_ref, sent_ref, blocks, taps,
):
    parity, inside = scalars[0], scalars[1] > 0
    chan_in, cells = 64, 128
    group = 9 * chan_in
    down_first = picker(2 * cells, 3 * 128, down_first_test)
    down_second = picker(192, 128, down_second_test)
    first = 0
    for part, planes, skip in ((below, 3, 4), (own, 4, 0), (above, 4, 0)):

        def row(r):
            lines = [
                part[(4 * p + r + skip) * chan_in : (4 * p + r + skip + 1) * chan_in, :]
                for p in range(planes)
            ]
            return jnp.concatenate(lines, 0)

        for b in range(3):
            if b == 0:
                picked = dot(row(1), down_first[cells:, :])
            else:
                picked = dot(jnp.concatenate([row(b - 1), row(b + 1)], 1), down_first)
            picked = picked.astype(BF)
            for p in range(planes):
                for e in range(3):
                    start = (first + p) * group + (3 * b + e) * chan_in
                    blocks[start : start + chan_in, :] = picked[
                        p * chan_in : (p + 1) * chan_in, e * 128 : (e + 1) * 128
                    ]
        first += planes
    quarter = 32
    lines = 16 * chan_in
    cotangent = jnp.concatenate(
        [
            part[lines + 16 * tile + 8 * half : lines + 16 * tile + 8 * half + 8, :].astype(F32)
            for half in range(2)
            for part in (own, above)
            for tile in range(4)
        ],
        0,
    )
    cotangent = jnp.concatenate([cotangent[:64], cotangent[64:]], 1)
    pres = []
    for h in range(5):
        if h == 3:
            pre = jnp.where(inside, dot(flipped[:, :group], blocks[6 * group : 7 * group, :]), 0.0)
            pre = pre + dot(flipped[:, group:], blocks[7 * group : 9 * group, :])
        else:
            pre = dot(flipped[...], blocks[2 * h * group : (2 * h + 3) * group, :])
        pres.append(pre)
        hidden = (pre * jax.nn.sigmoid(pre)).astype(BF)
        chan = hidden.shape[0]
        picked = dot_rows(down_second, hidden)
        for i in range(2):
            a = h - 2 * i
            if 0 <= a <= 2:
                masked = jnp.where(inside, picked, 0.0) if (i, a) == (1, 0) else picked
                masked = masked.astype(BF)
                for be in range(6):
                    taps[i * quarter : (i + 1) * quarter, (6 * a + be) * chan : (6 * a + be + 1) * chan] = (
                        masked[be * quarter : (be + 1) * quarter]
                    )
    pre = None
    for a in range(3):
        rows = second_weight[(9 * a + 3) * chan : 9 * (a + 1) * chan, :]
        term = dot(taps[:, 6 * a * chan : 6 * (a + 1) * chan], rows)
        pre = term if pre is None else pre + term
    ended = cotangent * gradient_silu(pre)
    delta = jnp.concatenate([ended[:quarter], jnp.where(inside, ended[quarter:], 0.0)], 0).T
    delta = delta.astype(BF)
    delta_ref[...] = delta
    for h in range(3):
        pre_ref[h] = pres[h + 1]
    share = 5 * chan
    ordered = dot(ended.astype(BF), picker(256, 256, reorder_test)).astype(BF)
    for ref, end in ((kept_ref, scalars[2]), (sent_ref, 1 - scalars[2])):
        start = pl.multiple_of((9 * parity + 4 * end) * chan, 128)
        ref[:, :share] = taps[:, pl.ds(start, share)]
        ref[:, share:] = ordered


def backward_kernel(
    scalars, below, own, delta_ref, pre_ref, first_weight, second_weight,
    volume_ref, kept_ref, sent_ref, grads,
):
    parity = scalars[0]
    chan_in, cells = 64, 128
    chan = pre_ref.shape[1]
    delta = delta_ref[...]
    up_first = picker(128, 768, up_first_test)
    up_second = picker(64, 1536, up_second_test)
    spread = dot(delta, up_second).astype(BF)
    lanes = spread.shape[1] // 12
    deltas = []
    for h, pairs in enumerate((((1, 0),), ((2, 0), (0, 1)), ((1, 1),))):
        total = None
        for a, i in pairs:
            for be in range(6):
                start = (9 * a + 3 + be) * chan
                term = dot(
                    second_weight[start : start + chan, :],
                    spread[:, (6 * i + be) * lanes : (6 * i + be + 1) * lanes],
                )
                total = term if total is None else total + term
        deltas.append((total * gradient_silu(pre_ref[h])).astype(BF))
    raised = dot(jnp.concatenate(deltas, 0), up_first).astype(BF)
    wide = 2 * cells
    stacks = [
        jnp.concatenate(
            [raised[h * chan : (h + 1) * chan, e * wide : (e + 1) * wide] for e in range(3)], 0
        )
        for h in range(3)
    ]

    def filters(a):
        return [
            jnp.concatenate([first_weight[9 * a + 3 * b + e] for e in range(3)], 1) for b in range(3)
        ]

    totals = {}
    for h, chosen in enumerate(((1, 2), (0, 1, 2), (0,))):
        left = jnp.concatenate(sum([filters(a) for a in chosen], []), 0)
        result = dot(left, stacks[h])
        for place, a in enumerate(chosen):
            p = 2 * h + a - 1
            for b in range(3):
                for j in range(2):
                    r = 2 * j + b - 1
                    if r < 0:
                        continue
                    start = (3 * place + b) * chan_in
                    term = result[start : start + chan_in, j * cells : (j + 1) * cells]
                    totals[p, r] = totals[p, r] + term if (p, r) in totals else term
    for (p, r), total in totals.items():
        volume_ref[p, r] = total.astype(BF)

    def plane(p, r):
        ref, start = (below, (12 + r) * chan_in) if p < 0 else (own, (4 * p + r) * chan_in)
        return ref[start : start + chan_in, :]

    blank = jnp.zeros((chan_in, cells), BF)
    lefts = []
    for a in range(3):
        for b in range(3):
            pieces = []
            for i in range(2):
                for j in range(2):
                    r = 2 * j + b - 1
                    pieces.append(blank if r < 0 else plane(2 * i + a - 1, r))
            lefts.append(jnp.concatenate(pieces, 1))
    result = dot_rows(jnp.concatenate(lefts, 0), jnp.concatenate(stacks[:2], 1))
    for ab in range(9):
        for e in range(3):
            start = (3 * ab + e) * chan_in
            grads[start : start + chan_in, :] = result[
                ab * chan_in : (ab + 1) * chan_in, e * chan : (e + 1) * chan
            ]
    grads[27 * chan_in :, :] = jnp.zeros((chan_in, chan), F32)
    samples_n, size = kept_ref.shape[:2]
    for m in range(samples_n):
        lower = grads[2 * m * size : (2 * m + 1) * size, :]
        upper = grads[(2 * m + 1) * size : (2 * m + 2) * size, :]
        kept_ref[m] = jnp.where(parity == 0, lower, upper).astype(BF)
        sent_ref[m] = jnp.where(parity == 0, upper, lower).astype(BF)


def second_kernel(mine, theirs, second_ref):
    chan = second_ref.shape[2]
    share = 5 * chan
    both = jnp.concatenate([mine[...], theirs[...]], 0)
    second = lax.dot_general(
        both[:, share:], both[:, :share], (((0,), (0,)), ((), ())), preferred_element_type=F32
    ).astype(BF)
    per = 32 // second_ref.shape[0]
    for piece in range(32):
        m, at = piece // per, piece % per * 40
        first = piece // 2 * 16
        for lane in range(2, 5) if piece % 2 else range(3):
            begin = first + 8 if lane == 2 and piece % 2 else first
            count = 8 if lane == 2 else 16
            second_ref[m, at : at + count, :] = second[
                begin : begin + count, lane * chan : (lane + 1) * chan
            ]
            at += count


def pack_kernel(second, kept, got, payload_ref):
    rows = second.shape[1]
    for m in range(kept.shape[0]):
        payload_ref[m, :rows, :] = second[m]
        total = kept[m].astype(F32) + got[m].astype(F32)
        payload_ref[m, rows:, :] = total.astype(BF)


def exchanged(parts, axis):
    return lax.all_to_all(parts, axis, split_axis=0, concat_axis=0, tiled=True)


def everywhere(value, axis):
    return exchanged(jnp.broadcast_to(value[None], (lax.axis_size(axis),) + value.shape), axis)


def shards(input_field, out_cotangent, first_weight, second_weight):
    chan_in, planes, height, length = input_field.shape[1:]
    chan_mid, chan_out = second_weight.shape[1:]
    groups = lax.axis_size("space")
    samples_n = lax.axis_size("sample")
    rows, half, quarter = (height // 2, length // 2, length // 4)
    per_group = chan_out // groups
    own = input_field[0].transpose(1, 2, 0, 3).reshape(-1, length)
    cotangent = out_cotangent[0].reshape(chan_out, quarter).T.reshape(4, 8, 2, 128)
    own = jnp.concatenate([own, cotangent.transpose(0, 2, 1, 3).reshape(64, 128)], 0)
    above = lax.ppermute(own, "space", [(i, (i - 1) % groups) for i in range(groups)])
    below = lax.ppermute(own, "space", [(i, i + 1) for i in range(groups - 1)])
    flipped = first_weight.reshape(27 * chan_in, chan_mid).T
    flat_second = second_weight.reshape(27 * chan_mid, chan_out)
    place = lax.axis_index("space")
    marks = [place % 2, jnp.where(place == groups - 1, 0, 1), place // 2 % 2]
    index = jnp.arange(3)
    scalars = jnp.where(index == 0, marks[0], jnp.where(index == 1, marks[1], marks[2]))
    scalars = scalars.astype(jnp.int32)
    size = 14 * chan_in // samples_n
    per = 32 // samples_n
    smem = pl.BlockSpec(memory_space=pltpu.SMEM)
    vmem = pl.BlockSpec(memory_space=pltpu.VMEM)
    swapped = jax.ShapeDtypeStruct((2 * quarter, 5 * chan_mid + chan_out), BF)
    halved = jax.ShapeDtypeStruct((samples_n, size, chan_mid), BF)
    pre, delta, mine, theirs = pl.pallas_call(
        forward_kernel,
        out_shape=(
            jax.ShapeDtypeStruct((3, chan_mid, rows * half), F32),
            jax.ShapeDtypeStruct((chan_out, 2 * quarter), BF),
            swapped,
            swapped,
        ),
        in_specs=[smem] + [vmem] * 5,
        scratch_shapes=[
            pltpu.VMEM((11 * 9 * chan_in, rows * half), BF),
            pltpu.VMEM((2 * quarter, 18 * chan_mid), BF),
        ],
        compiler_params=pltpu.CompilerParams(vmem_limit_bytes=16 << 20),
        cost_estimate=pl.CostEstimate(
            flops=2_000_000_000, bytes_accessed=5_000_000, transcendentals=0
        ),
    )(scalars, below, own, above, flipped, flat_second)
    theirs = lax.ppermute(theirs, "space", [(i, i ^ 2) for i in range(groups)])
    volume, kept, sent = pl.pallas_call(
        backward_kernel,
        out_shape=(
            jax.ShapeDtypeStruct((planes, height, chan_in, length), BF), halved, halved
        ),
        in_specs=[smem] + [vmem] * 6,
        scratch_shapes=[pltpu.VMEM((28 * chan_in, chan_mid), F32)],
        compiler_params=pltpu.CompilerParams(vmem_limit_bytes=16 << 20),
        cost_estimate=pl.CostEstimate(
            flops=3_000_000_000, bytes_accessed=5_000_000, transcendentals=0
        ),
    )(scalars, below, own, delta, pre, first_weight, flat_second)
    got = lax.ppermute(sent, "space", [(i, i ^ 1) for i in range(groups)])
    second = pl.pallas_call(
        second_kernel,
        out_shape=jax.ShapeDtypeStruct((samples_n, per * 40, chan_mid), BF),
        compiler_params=pltpu.CompilerParams(vmem_limit_bytes=8 << 20),
        cost_estimate=pl.CostEstimate(
            flops=2_000_000_000, bytes_accessed=2_000_000, transcendentals=0
        ),
    )(mine, theirs)
    payload = pl.pallas_call(
        pack_kernel,
        out_shape=jax.ShapeDtypeStruct((samples_n, per * 40 + size, chan_mid), BF),
        compiler_params=pltpu.CompilerParams(vmem_limit_bytes=8 << 20),
        cost_estimate=pl.CostEstimate(
            flops=50_000_000, bytes_accessed=2_000_000, transcendentals=0
        ),
    )(second, kept, got)
    input_grad = volume.transpose(2, 0, 1, 3)[None]
    chunk = jnp.sum(exchanged(payload, "sample").astype(F32), 0)
    first_chunk = jnp.broadcast_to(chunk[None, per * 40 :], (groups, size, chan_mid))
    second_chunk = chunk[: per * 40].reshape(per, 40, chan_mid)
    odd = (lax.axis_index("sample") * per + jnp.arange(per)) % 2 == 1
    second_chunk = jnp.where(
        odd[:, None, None],
        jnp.pad(second_chunk, ((0, 0), (8, 0), (0, 0))),
        jnp.pad(second_chunk, ((0, 0), (0, 8), (0, 0))),
    )
    pieces = 3 * per
    second_chunk = second_chunk.reshape(pieces, groups, chan_mid).transpose(1, 0, 2)
    second_chunk = jnp.pad(second_chunk, ((0, 0), (0, -(size + pieces) % 8), (0, 0)))
    both = exchanged(jnp.concatenate([first_chunk, second_chunk], 1).astype(BF), "space")
    both = both.astype(F32)
    first_chunk = jnp.sum(both[:, :size].reshape(groups // 2, 2, size, chan_mid), 0)
    second_chunk = both[:, size : size + pieces].reshape(groups // 4, 4, pieces, chan_mid)
    second_chunk = jnp.sum(second_chunk, 0)
    first_ext = planes // 2 * rows * half
    first_scale = 1.0 / math.sqrt(samples_n * groups * first_ext)
    second_scale = 1.0 / math.sqrt(samples_n * groups * (planes // 4) * (height // 4) * quarter)
    first_chunk = first_chunk.reshape(2 * size, chan_mid) * first_scale
    second_chunk = second_chunk.reshape(4 * pieces, chan_mid) * second_scale
    both = jnp.concatenate([first_chunk, second_chunk], 0)
    both = jnp.pad(both, ((0, -both.shape[0] % 8), (0, 0)))
    final = everywhere(both.astype(BF), "sample")
    first_grad = final[:, : 2 * size].reshape(28, chan_in, chan_mid)[:27]
    second = final[:, 2 * size : 2 * size + 4 * pieces].reshape(samples_n, 2, 2, per, 3, chan_mid)
    second = second.transpose(0, 3, 1, 2, 4, 5).reshape(per_group, 2, 2, 2, 3, chan_mid)
    second = second.transpose(1, 4, 2, 3, 0, 5)
    low, high = second[0], second[1]
    blocks = [low[0], low[1], low[2] + high[0], high[1], high[2]]
    second = jnp.stack([block[0] for block in blocks] + [block[1] for block in blocks[1:]], 1)
    second = second.reshape(3, 2, 3, per_group, chan_mid)
    second = jnp.pad(second, ((0, 0), (1, 0), (0, 0), (0, 0), (0, 0)))
    second_grad = second.reshape(27, per_group, chan_mid).transpose(0, 2, 1)
    return input_grad, first_grad, second_grad


def solution(mesh):
    placed = (
        P("sample", None, "space", None, None),
        P("sample", None, "space", None, None),
        P(),
        P(),
    )
    return jax.shard_map(
        shards,
        mesh=mesh,
        in_specs=placed,
        out_specs=(P("sample", None, "space", None, None), P(), P(None, None, "space")),
        check_vma=False,
    )
```

```python
import math

import jax
import jax.numpy as jnp
from jax import lax
from jax.experimental import pallas as pl
from jax.experimental.pallas import tpu as pltpu
from jax.sharding import PartitionSpec as P

BF = jnp.bfloat16
F32 = jnp.float32


def gradient_silu(values):
    logistic = jax.nn.sigmoid(values)
    return logistic * (1.0 + values * (1.0 - logistic))


def dot(left, right):
    return jnp.dot(left, right, preferred_element_type=F32)


def dot_rows(left, right):
    return lax.dot_general(left, right, (((1,), (1,)), ((), ())), preferred_element_type=F32)


def picker(rows, columns, test):
    r = lax.broadcasted_iota(jnp.int32, (rows, columns), 0)
    c = lax.broadcasted_iota(jnp.int32, (rows, columns), 1)
    return jnp.where(test(r, c), 1.0, 0.0).astype(BF)


def down_first_test(r, c):
    return ((r >> 7) == ((c >> 6) & 1)) & ((r & 127) == 2 * (c & 63) + (c >> 7) - 1)


def up_first_test(r, c):
    return ((r >> 6) == ((c >> 7) & 1)) & ((c & 127) == 2 * (r & 63) + (c >> 8) - 1)


def down_second_test(r, c):
    be = r >> 5
    b = jnp.where(be >= 3, 1, 0)
    return (b == (c >> 6)) & ((c & 63) == 2 * (r & 31) + be - 3 * b - 1)


def up_second_test(r, c):
    ibe = c >> 7
    i = jnp.where(ibe >= 6, 1, 0)
    be = ibe - 6 * i
    b = jnp.where(be >= 3, 1, 0)
    return ((r >> 5) == i) & (b == ((c >> 6) & 1)) & ((c & 63) == 2 * (r & 31) + be - 3 * b - 1)


def reorder_test(r, c):
    return ((r >> 4) == (c & 15)) & ((r & 15) == (c >> 4))


def forward_kernel(
    scalars, below, own, above, flipped, second_weight,
    pre_ref, delta_ref, kept_ref, sent_ref, blocks, taps,
):
    parity, inside = scalars[0], scalars[1] > 0
    chan_in, cells = 64, 128
    group = 9 * chan_in
    down_first = picker(2 * cells, 3 * 128, down_first_test)
    down_second = picker(192, 128, down_second_test)
    first = 0
    for part, planes, skip in ((below, 3, 4), (own, 4, 0), (above, 4, 0)):

        def row(r):
            lines = [
                part[(4 * p + r + skip) * chan_in : (4 * p + r + skip + 1) * chan_in, :]
                for p in range(planes)
            ]
            return jnp.concatenate(lines, 0)

        for b in range(3):
            if b == 0:
                picked = dot(row(1), down_first[cells:, :])
            else:
                picked = dot(jnp.concatenate([row(b - 1), row(b + 1)], 1), down_first)
            picked = picked.astype(BF)
            for p in range(planes):
                for e in range(3):
                    start = (first + p) * group + (3 * b + e) * chan_in
                    blocks[start : start + chan_in, :] = picked[
                        p * chan_in : (p + 1) * chan_in, e * 128 : (e + 1) * 128
                    ]
        first += planes
    quarter = 32
    lines = 16 * chan_in
    cotangent = jnp.concatenate(
        [
            part[lines + 16 * tile + 8 * half : lines + 16 * tile + 8 * half + 8, :].astype(F32)
            for half in range(2)
            for part in (own, above)
            for tile in range(4)
        ],
        0,
    )
    cotangent = jnp.concatenate([cotangent[:64], cotangent[64:]], 1)
    pres = []
    for h in range(5):
        if h == 3:
            pre = jnp.where(inside, dot(flipped[:, :group], blocks[6 * group : 7 * group, :]), 0.0)
            pre = pre + dot(flipped[:, group:], blocks[7 * group : 9 * group, :])
        else:
            pre = dot(flipped[...], blocks[2 * h * group : (2 * h + 3) * group, :])
        pres.append(pre)
        hidden = (pre * jax.nn.sigmoid(pre)).astype(BF)
        chan = hidden.shape[0]
        picked = dot_rows(down_second, hidden)
        for i in range(2):
            a = h - 2 * i
            if 0 <= a <= 2:
                masked = jnp.where(inside, picked, 0.0) if (i, a) == (1, 0) else picked
                masked = masked.astype(BF)
                for be in range(6):
                    taps[i * quarter : (i + 1) * quarter, (6 * a + be) * chan : (6 * a + be + 1) * chan] = (
                        masked[be * quarter : (be + 1) * quarter]
                    )
    pre = None
    for a in range(3):
        rows = second_weight[(9 * a + 3) * chan : 9 * (a + 1) * chan, :]
        term = dot(taps[:, 6 * a * chan : 6 * (a + 1) * chan], rows)
        pre = term if pre is None else pre + term
    ended = cotangent * gradient_silu(pre)
    delta = jnp.concatenate([ended[:quarter], jnp.where(inside, ended[quarter:], 0.0)], 0).T
    delta = delta.astype(BF)
    delta_ref[...] = delta
    for h in range(3):
        pre_ref[h] = pres[h + 1]
    share = 5 * chan
    ordered = dot(ended.astype(BF), picker(256, 256, reorder_test)).astype(BF)
    for ref, end in ((kept_ref, scalars[2]), (sent_ref, 1 - scalars[2])):
        start = pl.multiple_of((9 * parity + 4 * end) * chan, 128)
        ref[:, :share] = taps[:, pl.ds(start, share)]
        ref[:, share:] = ordered


def backward_kernel(
    scalars, below, own, delta_ref, pre_ref, first_weight, second_weight,
    volume_ref, kept_ref, sent_ref, grads,
):
    parity = scalars[0]
    chan_in, cells = 64, 128
    chan = pre_ref.shape[1]
    delta = delta_ref[...]
    up_first = picker(128, 768, up_first_test)
    up_second = picker(64, 1536, up_second_test)
    spread = dot(delta, up_second).astype(BF)
    lanes = spread.shape[1] // 12
    deltas = []
    for h, pairs in enumerate((((1, 0),), ((2, 0), (0, 1)), ((1, 1),))):
        total = None
        for a, i in pairs:
            for be in range(6):
                start = (9 * a + 3 + be) * chan
                term = dot(
                    second_weight[start : start + chan, :],
                    spread[:, (6 * i + be) * lanes : (6 * i + be + 1) * lanes],
                )
                total = term if total is None else total + term
        deltas.append((total * gradient_silu(pre_ref[h])).astype(BF))
    raised = dot(jnp.concatenate(deltas, 0), up_first).astype(BF)
    wide = 2 * cells
    stacks = [
        jnp.concatenate(
            [raised[h * chan : (h + 1) * chan, e * wide : (e + 1) * wide] for e in range(3)], 0
        )
        for h in range(3)
    ]

    def filters(a):
        return [
            jnp.concatenate([first_weight[9 * a + 3 * b + e] for e in range(3)], 1) for b in range(3)
        ]

    totals = {}
    for h, chosen in enumerate(((1, 2), (0, 1, 2), (0,))):
        left = jnp.concatenate(sum([filters(a) for a in chosen], []), 0)
        result = dot(left, stacks[h])
        for place, a in enumerate(chosen):
            p = 2 * h + a - 1
            for b in range(3):
                for j in range(2):
                    r = 2 * j + b - 1
                    if r < 0:
                        continue
                    start = (3 * place + b) * chan_in
                    term = result[start : start + chan_in, j * cells : (j + 1) * cells]
                    totals[p, r] = totals[p, r] + term if (p, r) in totals else term
    for (p, r), total in totals.items():
        volume_ref[p, r] = total.astype(BF)

    def plane(p, r):
        ref, start = (below, (12 + r) * chan_in) if p < 0 else (own, (4 * p + r) * chan_in)
        return ref[start : start + chan_in, :]

    blank = jnp.zeros((chan_in, cells), BF)
    lefts = []
    for a in range(3):
        for b in range(3):
            pieces = []
            for i in range(2):
                for j in range(2):
                    r = 2 * j + b - 1
                    pieces.append(blank if r < 0 else plane(2 * i + a - 1, r))
            lefts.append(jnp.concatenate(pieces, 1))
    result = dot_rows(jnp.concatenate(lefts, 0), jnp.concatenate(stacks[:2], 1))
    for ab in range(9):
        for e in range(3):
            start = (3 * ab + e) * chan_in
            grads[start : start + chan_in, :] = result[
                ab * chan_in : (ab + 1) * chan_in, e * chan : (e + 1) * chan
            ]
    grads[27 * chan_in :, :] = jnp.zeros((chan_in, chan), F32)
    samples_n, size = kept_ref.shape[:2]
    for m in range(samples_n):
        lower = grads[2 * m * size : (2 * m + 1) * size, :]
        upper = grads[(2 * m + 1) * size : (2 * m + 2) * size, :]
        kept_ref[m] = jnp.where(parity == 0, lower, upper).astype(BF)
        sent_ref[m] = jnp.where(parity == 0, upper, lower).astype(BF)


def second_kernel(mine, theirs, second_ref):
    chan = second_ref.shape[2]
    share = 5 * chan
    both = jnp.concatenate([mine[...], theirs[...]], 0)
    second = lax.dot_general(
        both[:, share:], both[:, :share], (((0,), (0,)), ((), ())), preferred_element_type=F32
    ).astype(BF)
    per = 32 // second_ref.shape[0]
    for piece in range(32):
        m, at = piece // per, piece % per * 40
        first = piece // 2 * 16
        for lane in range(2, 5) if piece % 2 else range(3):
            begin = first + 8 if lane == 2 and piece % 2 else first
            count = 8 if lane == 2 else 16
            second_ref[m, at : at + count, :] = second[
                begin : begin + count, lane * chan : (lane + 1) * chan
            ]
            at += count


def pack_kernel(second, kept, got, payload_ref):
    rows = second.shape[1]
    for m in range(kept.shape[0]):
        payload_ref[m, :rows, :] = second[m]
        total = kept[m].astype(F32) + got[m].astype(F32)
        payload_ref[m, rows:, :] = total.astype(BF)


def final_kernel(chunks, first_ref, second_ref):
    taps, chan_in, chan = first_ref.shape
    samples_n, rows = chunks.shape[0], chunks.shape[1] - 16
    for m in range(samples_n):
        at, stop = m * rows, min((m + 1) * rows, taps * chan_in)
        while at < stop:
            tap, channel = at // chan_in, at % chan_in
            count = min(stop - at, chan_in - channel)
            begin = 16 + at - m * rows
            first_ref[tap, channel : channel + count, :] = chunks[m, begin : begin + count, :]
            at += count
    per_group = second_ref.shape[1]

    def test(r, c):
        tap, o = r >> 4, r & 15
        q = jnp.where(tap >= 9, 1, 0)
        w = jnp.where(tap - 9 * q >= 5, 1, 0)
        block = tap - 9 * q - 4 * w - 2 * ((c >> 4) & 1)
        right = (block >= 0) & (block <= 2) & ((c & 15) == 6 * w + 3 * q + block)
        return right & ((c >> 5) == o)

    parts = jnp.concatenate([chunks[m, :16, :] for m in range(samples_n)], 0)
    live = dot(picker(18 * per_group, 16 * samples_n, test), parts).astype(BF)
    for a in range(3):
        for b in range(9):
            tap = 6 * a + b - 3
            value = live[tap * per_group : (tap + 1) * per_group]
            second_ref[9 * a + b] = jnp.zeros((per_group, chan), BF) if b < 3 else value


def exchanged(parts, axis):
    return lax.all_to_all(parts, axis, split_axis=0, concat_axis=0, tiled=True)


def everywhere(value, axis):
    return exchanged(jnp.broadcast_to(value[None], (lax.axis_size(axis),) + value.shape), axis)


def shards(input_field, out_cotangent, first_weight, second_weight):
    chan_in, planes, height, length = input_field.shape[1:]
    chan_mid, chan_out = second_weight.shape[1:]
    groups = lax.axis_size("space")
    samples_n = lax.axis_size("sample")
    rows, half, quarter = (height // 2, length // 2, length // 4)
    per_group = chan_out // groups
    own = input_field[0].transpose(1, 2, 0, 3).reshape(-1, length)
    cotangent = out_cotangent[0].reshape(chan_out, quarter).T.reshape(4, 8, 2, 128)
    own = jnp.concatenate([own, cotangent.transpose(0, 2, 1, 3).reshape(64, 128)], 0)
    above = lax.ppermute(own, "space", [(i, (i - 1) % groups) for i in range(groups)])
    below = lax.ppermute(own, "space", [(i, i + 1) for i in range(groups - 1)])
    flipped = first_weight.reshape(27 * chan_in, chan_mid).T
    flat_second = second_weight.reshape(27 * chan_mid, chan_out)
    place = lax.axis_index("space")
    marks = [place % 2, jnp.where(place == groups - 1, 0, 1), place // 2 % 2]
    index = jnp.arange(3)
    scalars = jnp.where(index == 0, marks[0], jnp.where(index == 1, marks[1], marks[2]))
    scalars = scalars.astype(jnp.int32)
    size = 14 * chan_in // samples_n
    per = 32 // samples_n
    smem = pl.BlockSpec(memory_space=pltpu.SMEM)
    vmem = pl.BlockSpec(memory_space=pltpu.VMEM)
    swapped = jax.ShapeDtypeStruct((2 * quarter, 5 * chan_mid + chan_out), BF)
    halved = jax.ShapeDtypeStruct((samples_n, size, chan_mid), BF)
    pre, delta, mine, theirs = pl.pallas_call(
        forward_kernel,
        out_shape=(
            jax.ShapeDtypeStruct((3, chan_mid, rows * half), F32),
            jax.ShapeDtypeStruct((chan_out, 2 * quarter), BF),
            swapped,
            swapped,
        ),
        in_specs=[smem] + [vmem] * 5,
        scratch_shapes=[
            pltpu.VMEM((11 * 9 * chan_in, rows * half), BF),
            pltpu.VMEM((2 * quarter, 18 * chan_mid), BF),
        ],
        compiler_params=pltpu.CompilerParams(vmem_limit_bytes=16 << 20),
        cost_estimate=pl.CostEstimate(
            flops=2_000_000_000, bytes_accessed=5_000_000, transcendentals=0
        ),
    )(scalars, below, own, above, flipped, flat_second)
    theirs = lax.ppermute(theirs, "space", [(i, i ^ 2) for i in range(groups)])
    volume, kept, sent = pl.pallas_call(
        backward_kernel,
        out_shape=(
            jax.ShapeDtypeStruct((planes, height, chan_in, length), BF), halved, halved
        ),
        in_specs=[smem] + [vmem] * 6,
        scratch_shapes=[pltpu.VMEM((28 * chan_in, chan_mid), F32)],
        compiler_params=pltpu.CompilerParams(vmem_limit_bytes=16 << 20),
        cost_estimate=pl.CostEstimate(
            flops=3_000_000_000, bytes_accessed=5_000_000, transcendentals=0
        ),
    )(scalars, below, own, delta, pre, first_weight, flat_second)
    got = lax.ppermute(sent, "space", [(i, i ^ 1) for i in range(groups)])
    second = pl.pallas_call(
        second_kernel,
        out_shape=jax.ShapeDtypeStruct((samples_n, per * 40, chan_mid), BF),
        compiler_params=pltpu.CompilerParams(vmem_limit_bytes=8 << 20),
        cost_estimate=pl.CostEstimate(
            flops=2_000_000_000, bytes_accessed=2_000_000, transcendentals=0
        ),
    )(mine, theirs)
    payload = pl.pallas_call(
        pack_kernel,
        out_shape=jax.ShapeDtypeStruct((samples_n, per * 40 + size, chan_mid), BF),
        compiler_params=pltpu.CompilerParams(vmem_limit_bytes=8 << 20),
        cost_estimate=pl.CostEstimate(
            flops=50_000_000, bytes_accessed=2_000_000, transcendentals=0
        ),
    )(second, kept, got)
    input_grad = volume.transpose(2, 0, 1, 3)[None]
    chunk = jnp.sum(exchanged(payload, "sample").astype(F32), 0)
    first_chunk = jnp.broadcast_to(chunk[None, per * 40 :], (groups, size, chan_mid))
    second_chunk = chunk[: per * 40].reshape(per, 40, chan_mid)
    odd = (lax.axis_index("sample") * per + jnp.arange(per)) % 2 == 1
    second_chunk = jnp.where(
        odd[:, None, None],
        jnp.pad(second_chunk, ((0, 0), (8, 0), (0, 0))),
        jnp.pad(second_chunk, ((0, 0), (0, 8), (0, 0))),
    )
    pieces = 3 * per
    second_chunk = second_chunk.reshape(pieces, groups, chan_mid).transpose(1, 0, 2)
    second_chunk = jnp.pad(second_chunk, ((0, 0), (0, -(size + pieces) % 8), (0, 0)))
    both = exchanged(jnp.concatenate([first_chunk, second_chunk], 1).astype(BF), "space")
    both = both.astype(F32)
    first_chunk = jnp.sum(both[:, :size].reshape(groups // 2, 2, size, chan_mid), 0)
    second_chunk = both[:, size : size + pieces].reshape(groups // 4, 4, pieces, chan_mid)
    second_chunk = jnp.sum(second_chunk, 0)
    first_ext = planes // 2 * rows * half
    first_scale = 1.0 / math.sqrt(samples_n * groups * first_ext)
    second_scale = 1.0 / math.sqrt(samples_n * groups * (planes // 4) * (height // 4) * quarter)
    first_chunk = first_chunk.reshape(2 * size, chan_mid) * first_scale
    second_chunk = second_chunk.reshape(4 * pieces, chan_mid) * second_scale
    second_chunk = jnp.pad(second_chunk, ((0, 16 - 4 * pieces), (0, 0)))
    both = jnp.concatenate([second_chunk, first_chunk], 0).astype(BF)
    first_grad, second_grad = pl.pallas_call(
        final_kernel,
        out_shape=(
            jax.ShapeDtypeStruct((27, chan_in, chan_mid), BF),
            jax.ShapeDtypeStruct((27, per_group, chan_mid), BF),
        ),
        compiler_params=pltpu.CompilerParams(vmem_limit_bytes=8 << 20),
        cost_estimate=pl.CostEstimate(
            flops=40_000_000, bytes_accessed=1_200_000, transcendentals=0
        ),
    )(everywhere(both, "sample"))
    second_grad = second_grad.transpose(0, 2, 1)
    return input_grad, first_grad, second_grad


def solution(mesh):
    placed = (
        P("sample", None, "space", None, None),
        P("sample", None, "space", None, None),
        P(),
        P(),
    )
    return jax.shard_map(
        shards,
        mesh=mesh,
        in_specs=placed,
        out_specs=(P("sample", None, "space", None, None), P(), P(None, None, "space")),
        check_vma=False,
    )
```

```python
import math

import jax
import jax.numpy as jnp
from jax import lax
from jax.experimental import pallas as pl
from jax.experimental.pallas import tpu as pltpu
from jax.sharding import PartitionSpec as P

BF = jnp.bfloat16
F32 = jnp.float32


def gradient_silu(values):
    logistic = jax.nn.sigmoid(values)
    return logistic * (1.0 + values * (1.0 - logistic))


def dot(left, right):
    return jnp.dot(left, right, preferred_element_type=F32)


def dot_rows(left, right):
    return lax.dot_general(left, right, (((1,), (1,)), ((), ())), preferred_element_type=F32)


def picker(rows, columns, test):
    r = lax.broadcasted_iota(jnp.int32, (rows, columns), 0)
    c = lax.broadcasted_iota(jnp.int32, (rows, columns), 1)
    return jnp.where(test(r, c), 1.0, 0.0).astype(BF)


def down_first_test(r, c):
    return ((r >> 7) == ((c >> 6) & 1)) & ((r & 127) == 2 * (c & 63) + (c >> 7) - 1)


def up_first_test(r, c):
    return ((r >> 6) == ((c >> 7) & 1)) & ((c & 127) == 2 * (r & 63) + (c >> 8) - 1)


def down_second_test(r, c):
    be = r >> 5
    b = jnp.where(be >= 3, 1, 0)
    return (b == (c >> 6)) & ((c & 63) == 2 * (r & 31) + be - 3 * b - 1)


def up_second_test(r, c):
    ibe = c >> 7
    i = jnp.where(ibe >= 6, 1, 0)
    be = ibe - 6 * i
    b = jnp.where(be >= 3, 1, 0)
    return ((r >> 5) == i) & (b == ((c >> 6) & 1)) & ((c & 63) == 2 * (r & 31) + be - 3 * b - 1)


def reorder_test(r, c):
    return ((r >> 4) == (c & 15)) & ((r & 15) == (c >> 4))


def forward_kernel(
    scalars, below, own, above, flipped, second_weight,
    pre_ref, delta_ref, kept_ref, sent_ref, blocks, taps,
):
    parity, inside = scalars[0], scalars[1] > 0
    chan_in, cells = 64, 128
    group = 9 * chan_in
    down_first = picker(2 * cells, 3 * 128, down_first_test)
    down_second = picker(192, 128, down_second_test)
    first = 0
    for part, planes, skip in ((below, 3, 4), (own, 4, 0), (above, 4, 0)):

        def row(r):
            lines = [
                part[(4 * p + r + skip) * chan_in : (4 * p + r + skip + 1) * chan_in, :]
                for p in range(planes)
            ]
            return jnp.concatenate(lines, 0)

        for b in range(3):
            if b == 0:
                picked = dot(row(1), down_first[cells:, :])
            else:
                picked = dot(jnp.concatenate([row(b - 1), row(b + 1)], 1), down_first)
            picked = picked.astype(BF)
            for p in range(planes):
                for e in range(3):
                    value = picked[p * chan_in : (p + 1) * chan_in, e * 128 : (e + 1) * 128]
                    for a in range(3):
                        h, odd = (first + p - a) // 2, (first + p - a) % 2
                        if odd or not 0 <= h <= 4:
                            continue
                        placed = value
                        if (a, h) == (0, 3):
                            placed = jnp.where(inside, value.astype(F32), 0.0).astype(BF)
                        start = a * group + (3 * b + e) * chan_in
                        blocks[start : start + chan_in, h * 128 : (h + 1) * 128] = placed
        first += planes
    quarter = 32
    lines = 16 * chan_in
    cotangent = jnp.concatenate(
        [
            part[lines + 16 * tile + 8 * half : lines + 16 * tile + 8 * half + 8, :].astype(F32)
            for half in range(2)
            for part in (own, above)
            for tile in range(4)
        ],
        0,
    )
    cotangent = jnp.concatenate([cotangent[:64], cotangent[64:]], 1)
    pres = []
    wide = dot(flipped[...], blocks[...])
    for h in range(5):
        pre = wide[:, h * 128 : (h + 1) * 128]
        pres.append(pre)
        hidden = (pre * jax.nn.sigmoid(pre)).astype(BF)
        chan = hidden.shape[0]
        picked = dot_rows(down_second, hidden)
        for i in range(2):
            a = h - 2 * i
            if 0 <= a <= 2:
                masked = jnp.where(inside, picked, 0.0) if (i, a) == (1, 0) else picked
                masked = masked.astype(BF)
                for be in range(6):
                    taps[i * quarter : (i + 1) * quarter, (6 * a + be) * chan : (6 * a + be + 1) * chan] = (
                        masked[be * quarter : (be + 1) * quarter]
                    )
    pre = None
    for a in range(3):
        rows = second_weight[(9 * a + 3) * chan : 9 * (a + 1) * chan, :]
        term = dot(taps[:, 6 * a * chan : 6 * (a + 1) * chan], rows)
        pre = term if pre is None else pre + term
    ended = cotangent * gradient_silu(pre)
    delta = jnp.concatenate([ended[:quarter], jnp.where(inside, ended[quarter:], 0.0)], 0).T
    delta = delta.astype(BF)
    delta_ref[...] = delta
    for h in range(3):
        pre_ref[h] = pres[h + 1]
    share = 5 * chan
    ordered = dot(ended.astype(BF), picker(256, 256, reorder_test)).astype(BF)
    for ref, end in ((kept_ref, scalars[2]), (sent_ref, 1 - scalars[2])):
        start = pl.multiple_of((9 * parity + 4 * end) * chan, 128)
        ref[:, :share] = taps[:, pl.ds(start, share)]
        ref[:, share:] = ordered


def backward_kernel(
    scalars, below, own, delta_ref, pre_ref, second_weight,
    stacks_ref, kept_ref, sent_ref, grads,
):
    parity = scalars[0]
    chan_in, cells = 64, 128
    chan = pre_ref.shape[1]
    delta = delta_ref[...]
    up_first = picker(128, 768, up_first_test)
    up_second = picker(64, 1536, up_second_test)
    spread = dot(delta, up_second).astype(BF)
    lanes = spread.shape[1] // 12
    deltas = []
    for h, pairs in enumerate((((1, 0),), ((2, 0), (0, 1)), ((1, 1),))):
        total = None
        for a, i in pairs:
            for be in range(6):
                start = (9 * a + 3 + be) * chan
                term = dot(
                    second_weight[start : start + chan, :],
                    spread[:, (6 * i + be) * lanes : (6 * i + be + 1) * lanes],
                )
                total = term if total is None else total + term
        deltas.append((total * gradient_silu(pre_ref[h])).astype(BF))
    raised = dot(jnp.concatenate(deltas, 0), up_first).astype(BF)
    wide = 2 * cells
    stacks = [
        jnp.concatenate(
            [raised[h * chan : (h + 1) * chan, e * wide : (e + 1) * wide] for e in range(3)], 0
        )
        for h in range(3)
    ]

    for h in range(3):
        stacks_ref[h] = stacks[h]

    def plane(p, r):
        ref, start = (below, (12 + r) * chan_in) if p < 0 else (own, (4 * p + r) * chan_in)
        return ref[start : start + chan_in, :]

    blank = jnp.zeros((chan_in, cells), BF)
    lefts = []
    for a in range(3):
        for b in range(3):
            pieces = []
            for i in range(2):
                for j in range(2):
                    r = 2 * j + b - 1
                    pieces.append(blank if r < 0 else plane(2 * i + a - 1, r))
            lefts.append(jnp.concatenate(pieces, 1))
    result = dot_rows(jnp.concatenate(lefts, 0), jnp.concatenate(stacks[:2], 1))
    for ab in range(9):
        for e in range(3):
            start = (3 * ab + e) * chan_in
            grads[start : start + chan_in, :] = result[
                ab * chan_in : (ab + 1) * chan_in, e * chan : (e + 1) * chan
            ]
    grads[27 * chan_in :, :] = jnp.zeros((chan_in, chan), F32)
    samples_n, size = kept_ref.shape[:2]
    for m in range(samples_n):
        lower = grads[2 * m * size : (2 * m + 1) * size, :]
        upper = grads[(2 * m + 1) * size : (2 * m + 2) * size, :]
        kept_ref[m] = jnp.where(parity == 0, lower, upper).astype(BF)
        sent_ref[m] = jnp.where(parity == 0, upper, lower).astype(BF)


def middle_kernel(mine, theirs, stacks, first_weight, second_ref, volume_ref):
    chan_in, cells = volume_ref.shape[2:]
    chan = second_ref.shape[2]
    def filters(a):
        return [
            jnp.concatenate([first_weight[9 * a + 3 * b + e] for e in range(3)], 1) for b in range(3)
        ]

    totals = {}
    for h, chosen in enumerate(((1, 2), (0, 1, 2), (0,))):
        left = jnp.concatenate(sum([filters(a) for a in chosen], []), 0)
        result = dot(left, stacks[h])
        for place, a in enumerate(chosen):
            p = 2 * h + a - 1
            for b in range(3):
                for j in range(2):
                    r = 2 * j + b - 1
                    if r < 0:
                        continue
                    start = (3 * place + b) * chan_in
                    term = result[start : start + chan_in, j * cells : (j + 1) * cells]
                    totals[p, r] = totals[p, r] + term if (p, r) in totals else term
    for (p, r), total in totals.items():
        volume_ref[p, r] = total.astype(BF)

    share = 5 * chan
    both = jnp.concatenate([mine[...], theirs[...]], 0)
    second = lax.dot_general(
        both[:, share:], both[:, :share], (((0,), (0,)), ((), ())), preferred_element_type=F32
    ).astype(BF)
    per = 32 // second_ref.shape[0]
    for piece in range(32):
        m, at = piece // per, piece % per * 40
        first = piece // 2 * 16
        for lane in range(2, 5) if piece % 2 else range(3):
            begin = first + 8 if lane == 2 and piece % 2 else first
            count = 8 if lane == 2 else 16
            second_ref[m, at : at + count, :] = second[
                begin : begin + count, lane * chan : (lane + 1) * chan
            ]
            at += count


def pack_kernel(second, kept, got, payload_ref):
    rows = second.shape[1]
    for m in range(kept.shape[0]):
        payload_ref[m, :rows, :] = second[m]
        total = kept[m].astype(F32) + got[m].astype(F32)
        payload_ref[m, rows:, :] = total.astype(BF)


def final_kernel(chunks, first_ref, second_ref):
    taps, chan_in, chan = first_ref.shape
    samples_n, rows = chunks.shape[0], chunks.shape[1] - 16
    for m in range(samples_n):
        at, stop = m * rows, min((m + 1) * rows, taps * chan_in)
        while at < stop:
            tap, channel = at // chan_in, at % chan_in
            count = min(stop - at, chan_in - channel)
            begin = 16 + at - m * rows
            first_ref[tap, channel : channel + count, :] = chunks[m, begin : begin + count, :]
            at += count
    per_group = second_ref.shape[1]

    def test(r, c):
        tap, o = r >> 4, r & 15
        q = jnp.where(tap >= 9, 1, 0)
        w = jnp.where(tap - 9 * q >= 5, 1, 0)
        block = tap - 9 * q - 4 * w - 2 * ((c >> 4) & 1)
        right = (block >= 0) & (block <= 2) & ((c & 15) == 6 * w + 3 * q + block)
        return right & ((c >> 5) == o)

    parts = jnp.concatenate([chunks[m, :16, :] for m in range(samples_n)], 0)
    live = dot(picker(18 * per_group, 16 * samples_n, test), parts).astype(BF)
    for a in range(3):
        for b in range(9):
            tap = 6 * a + b - 3
            value = live[tap * per_group : (tap + 1) * per_group]
            second_ref[9 * a + b] = jnp.zeros((per_group, chan), BF) if b < 3 else value


def exchanged(parts, axis):
    return lax.all_to_all(parts, axis, split_axis=0, concat_axis=0, tiled=True)


def everywhere(value, axis):
    return exchanged(jnp.broadcast_to(value[None], (lax.axis_size(axis),) + value.shape), axis)


def shards(input_field, out_cotangent, first_weight, second_weight):
    chan_in, planes, height, length = input_field.shape[1:]
    chan_mid, chan_out = second_weight.shape[1:]
    groups = lax.axis_size("space")
    samples_n = lax.axis_size("sample")
    rows, half, quarter = (height // 2, length // 2, length // 4)
    per_group = chan_out // groups
    own = input_field[0].transpose(1, 2, 0, 3).reshape(-1, length)
    cotangent = out_cotangent[0].reshape(chan_out, quarter).T.reshape(4, 8, 2, 128)
    own = jnp.concatenate([own, cotangent.transpose(0, 2, 1, 3).reshape(64, 128)], 0)
    above = lax.ppermute(own, "space", [(i, (i - 1) % groups) for i in range(groups)])
    below = lax.ppermute(own, "space", [(i, i + 1) for i in range(groups - 1)])
    flipped = first_weight.reshape(27 * chan_in, chan_mid).T
    flat_second = second_weight.reshape(27 * chan_mid, chan_out)
    place = lax.axis_index("space")
    marks = [place % 2, jnp.where(place == groups - 1, 0, 1), place // 2 % 2]
    index = jnp.arange(3)
    scalars = jnp.where(index == 0, marks[0], jnp.where(index == 1, marks[1], marks[2]))
    scalars = scalars.astype(jnp.int32)
    size = 14 * chan_in // samples_n
    per = 32 // samples_n
    smem = pl.BlockSpec(memory_space=pltpu.SMEM)
    vmem = pl.BlockSpec(memory_space=pltpu.VMEM)
    swapped = jax.ShapeDtypeStruct((2 * quarter, 5 * chan_mid + chan_out), BF)
    halved = jax.ShapeDtypeStruct((samples_n, size, chan_mid), BF)
    pre, delta, mine, theirs = pl.pallas_call(
        forward_kernel,
        out_shape=(
            jax.ShapeDtypeStruct((3, chan_mid, rows * half), F32),
            jax.ShapeDtypeStruct((chan_out, 2 * quarter), BF),
            swapped,
            swapped,
        ),
        in_specs=[smem] + [vmem] * 5,
        scratch_shapes=[
            pltpu.VMEM((27 * chan_in, 5 * rows * half), BF),
            pltpu.VMEM((2 * quarter, 18 * chan_mid), BF),
        ],
        compiler_params=pltpu.CompilerParams(vmem_limit_bytes=16 << 20),
        cost_estimate=pl.CostEstimate(
            flops=2_000_000_000, bytes_accessed=5_000_000, transcendentals=0
        ),
    )(scalars, below, own, above, flipped, flat_second)
    theirs = lax.ppermute(theirs, "space", [(i, i ^ 2) for i in range(groups)])
    stacks, kept, sent = pl.pallas_call(
        backward_kernel,
        out_shape=(jax.ShapeDtypeStruct((3, 3 * chan_mid, 2 * length), BF), halved, halved),
        in_specs=[smem] + [vmem] * 5,
        scratch_shapes=[pltpu.VMEM((28 * chan_in, chan_mid), F32)],
        compiler_params=pltpu.CompilerParams(vmem_limit_bytes=16 << 20),
        cost_estimate=pl.CostEstimate(
            flops=3_000_000_000, bytes_accessed=5_000_000, transcendentals=0
        ),
    )(scalars, below, own, delta, pre, flat_second)
    got = lax.ppermute(sent, "space", [(i, i ^ 1) for i in range(groups)])
    second, volume = pl.pallas_call(
        middle_kernel,
        out_shape=(
            jax.ShapeDtypeStruct((samples_n, per * 40, chan_mid), BF),
            jax.ShapeDtypeStruct((planes, height, chan_in, length), BF),
        ),
        compiler_params=pltpu.CompilerParams(vmem_limit_bytes=8 << 20),
        cost_estimate=pl.CostEstimate(
            flops=2_000_000_000, bytes_accessed=2_000_000, transcendentals=0
        ),
    )(mine, theirs, stacks, first_weight)
    payload = pl.pallas_call(
        pack_kernel,
        out_shape=jax.ShapeDtypeStruct((samples_n, per * 40 + size, chan_mid), BF),
        compiler_params=pltpu.CompilerParams(vmem_limit_bytes=8 << 20),
        cost_estimate=pl.CostEstimate(
            flops=50_000_000, bytes_accessed=2_000_000, transcendentals=0
        ),
    )(second, kept, got)
    input_grad = volume.transpose(2, 0, 1, 3)[None]
    chunk = jnp.sum(exchanged(payload, "sample").astype(F32), 0)
    first_chunk = jnp.broadcast_to(chunk[None, per * 40 :], (groups, size, chan_mid))
    second_chunk = chunk[: per * 40].reshape(per, 40, chan_mid)
    odd = (lax.axis_index("sample") * per + jnp.arange(per)) % 2 == 1
    second_chunk = jnp.where(
        odd[:, None, None],
        jnp.pad(second_chunk, ((0, 0), (8, 0), (0, 0))),
        jnp.pad(second_chunk, ((0, 0), (0, 8), (0, 0))),
    )
    pieces = 3 * per
    second_chunk = second_chunk.reshape(pieces, groups, chan_mid).transpose(1, 0, 2)
    second_chunk = jnp.pad(second_chunk, ((0, 0), (0, -(size + pieces) % 8), (0, 0)))
    both = exchanged(jnp.concatenate([first_chunk, second_chunk], 1).astype(BF), "space")
    both = both.astype(F32)
    first_chunk = jnp.sum(both[:, :size].reshape(groups // 2, 2, size, chan_mid), 0)
    second_chunk = both[:, size : size + pieces].reshape(groups // 4, 4, pieces, chan_mid)
    second_chunk = jnp.sum(second_chunk, 0)
    first_ext = planes // 2 * rows * half
    first_scale = 1.0 / math.sqrt(samples_n * groups * first_ext)
    second_scale = 1.0 / math.sqrt(samples_n * groups * (planes // 4) * (height // 4) * quarter)
    first_chunk = first_chunk.reshape(2 * size, chan_mid) * first_scale
    second_chunk = second_chunk.reshape(4 * pieces, chan_mid) * second_scale
    second_chunk = jnp.pad(second_chunk, ((0, 16 - 4 * pieces), (0, 0)))
    both = jnp.concatenate([second_chunk, first_chunk], 0).astype(BF)
    first_grad, second_grad = pl.pallas_call(
        final_kernel,
        out_shape=(
            jax.ShapeDtypeStruct((27, chan_in, chan_mid), BF),
            jax.ShapeDtypeStruct((27, per_group, chan_mid), BF),
        ),
        compiler_params=pltpu.CompilerParams(vmem_limit_bytes=8 << 20),
        cost_estimate=pl.CostEstimate(
            flops=40_000_000, bytes_accessed=1_200_000, transcendentals=0
        ),
    )(everywhere(both, "sample"))
    second_grad = second_grad.transpose(0, 2, 1)
    return input_grad, first_grad, second_grad


def solution(mesh):
    placed = (
        P("sample", None, "space", None, None),
        P("sample", None, "space", None, None),
        P(),
        P(),
    )
    return jax.shard_map(
        shards,
        mesh=mesh,
        in_specs=placed,
        out_specs=(P("sample", None, "space", None, None), P(), P(None, None, "space")),
        check_vma=False,
    )
```

```python
import math

import jax
import jax.numpy as jnp
from jax import lax
from jax.experimental import pallas as pl
from jax.experimental.pallas import tpu as pltpu
from jax.sharding import PartitionSpec as P

BF = jnp.bfloat16
F32 = jnp.float32


def gradient_silu(values):
    logistic = jax.nn.sigmoid(values)
    return logistic * (1.0 + values * (1.0 - logistic))


def dot(left, right):
    return jnp.dot(left, right, preferred_element_type=F32)


def dot_rows(left, right):
    return lax.dot_general(left, right, (((1,), (1,)), ((), ())), preferred_element_type=F32)


def picker(rows, columns, test):
    r = lax.broadcasted_iota(jnp.int32, (rows, columns), 0)
    c = lax.broadcasted_iota(jnp.int32, (rows, columns), 1)
    return jnp.where(test(r, c), 1.0, 0.0).astype(BF)


def down_first_test(r, c):
    return ((r >> 7) == ((c >> 6) & 1)) & ((r & 127) == 2 * (c & 63) + (c >> 7) - 1)


def up_first_test(r, c):
    return ((r >> 6) == ((c >> 7) & 1)) & ((c & 127) == 2 * (r & 63) + (c >> 8) - 1)


def down_second_test(r, c):
    be = r >> 5
    b = jnp.where(be >= 3, 1, 0)
    return (b == (c >> 6)) & ((c & 63) == 2 * (r & 31) + be - 3 * b - 1)


def up_second_test(r, c):
    ibe = c >> 7
    i = jnp.where(ibe >= 6, 1, 0)
    be = ibe - 6 * i
    b = jnp.where(be >= 3, 1, 0)
    return ((r >> 5) == i) & (b == ((c >> 6) & 1)) & ((c & 63) == 2 * (r & 31) + be - 3 * b - 1)


def reorder_test(r, c):
    return ((r >> 4) == (c & 15)) & ((r & 15) == (c >> 4))


def forward_kernel(
    scalars, below, own, above, flipped, second_weight,
    pre_ref, delta_ref, kept_ref, sent_ref, blocks, taps,
):
    parity, inside = scalars[0], scalars[1] > 0
    chan_in, cells = 64, 128
    group = 9 * chan_in
    down_first = picker(2 * cells, 3 * 128, down_first_test)
    down_second = picker(192, 128, down_second_test)
    first = 0
    for part, planes, skip in ((below, 3, 4), (own, 4, 0), (above, 4, 0)):

        def row(r):
            lines = [
                part[(4 * p + r + skip) * chan_in : (4 * p + r + skip + 1) * chan_in, :]
                for p in range(planes)
            ]
            return jnp.concatenate(lines, 0)

        for b in range(3):
            if b == 0:
                picked = dot(row(1), down_first[cells:, :])
            else:
                picked = dot(jnp.concatenate([row(b - 1), row(b + 1)], 1), down_first)
            picked = picked.astype(BF)
            for p in range(planes):
                for e in range(3):
                    value = picked[p * chan_in : (p + 1) * chan_in, e * 128 : (e + 1) * 128]
                    for a in range(3):
                        h, odd = (first + p - a) // 2, (first + p - a) % 2
                        if odd or not 0 <= h <= 4:
                            continue
                        placed = value
                        if (a, h) == (0, 3):
                            placed = jnp.where(inside, value.astype(F32), 0.0).astype(BF)
                        start = a * group + (3 * b + e) * chan_in
                        blocks[start : start + chan_in, h * 128 : (h + 1) * 128] = placed
        first += planes
    quarter = 32
    lines = 16 * chan_in
    cotangent = jnp.concatenate(
        [
            part[lines + 16 * tile + 8 * half : lines + 16 * tile + 8 * half + 8, :].astype(F32)
            for half in range(2)
            for part in (own, above)
            for tile in range(4)
        ],
        0,
    )
    cotangent = jnp.concatenate([cotangent[:64], cotangent[64:]], 1)
    pres = []
    wide = dot(flipped[...], blocks[...])
    for h in range(5):
        pre = wide[:, h * 128 : (h + 1) * 128]
        pres.append(pre)
        hidden = (pre * jax.nn.sigmoid(pre)).astype(BF)
        chan = hidden.shape[0]
        picked = dot_rows(down_second, hidden)
        for i in range(2):
            a = h - 2 * i
            if 0 <= a <= 2:
                masked = jnp.where(inside, picked, 0.0) if (i, a) == (1, 0) else picked
                masked = masked.astype(BF)
                for be in range(6):
                    taps[i * quarter : (i + 1) * quarter, (6 * a + be) * chan : (6 * a + be + 1) * chan] = (
                        masked[be * quarter : (be + 1) * quarter]
                    )
    pre = None
    for a in range(3):
        rows = second_weight[(9 * a + 3) * chan : 9 * (a + 1) * chan, :]
        term = dot(taps[:, 6 * a * chan : 6 * (a + 1) * chan], rows)
        pre = term if pre is None else pre + term
    ended = cotangent * gradient_silu(pre)
    delta = jnp.concatenate([ended[:quarter], jnp.where(inside, ended[quarter:], 0.0)], 0).T
    delta = delta.astype(BF)
    delta_ref[...] = delta
    for h in range(3):
        pre_ref[h] = pres[h + 1]
    share = 5 * chan
    ordered = dot(ended.astype(BF), picker(256, 256, reorder_test)).astype(BF)
    for ref, end in ((kept_ref, scalars[2]), (sent_ref, 1 - scalars[2])):
        start = pl.multiple_of((9 * parity + 4 * end) * chan, 128)
        ref[:, :share] = taps[:, pl.ds(start, share)]
        ref[:, share:] = ordered


def backward_kernel(
    scalars, below, own, delta_ref, pre_ref, second_weight,
    stacks_ref, kept_ref, sent_ref, grads,
):
    parity = scalars[0]
    chan_in, cells = 64, 128
    chan = pre_ref.shape[1]
    delta = delta_ref[...]
    up_first = picker(128, 768, up_first_test)
    up_second = picker(64, 1536, up_second_test)
    spread = dot(delta, up_second).astype(BF)
    lanes = spread.shape[1] // 12
    deltas = []
    for h, pairs in enumerate((((1, 0),), ((2, 0), (0, 1)), ((1, 1),))):
        total = None
        for a, i in pairs:
            for be in range(6):
                start = (9 * a + 3 + be) * chan
                term = dot(
                    second_weight[start : start + chan, :],
                    spread[:, (6 * i + be) * lanes : (6 * i + be + 1) * lanes],
                )
                total = term if total is None else total + term
        deltas.append((total * gradient_silu(pre_ref[h])).astype(BF))
    raised = dot(jnp.concatenate(deltas, 0), up_first).astype(BF)
    wide = 2 * cells
    stacks = [
        jnp.concatenate(
            [raised[h * chan : (h + 1) * chan, e * wide : (e + 1) * wide] for e in range(3)], 0
        )
        for h in range(3)
    ]

    for h in range(3):
        stacks_ref[h] = stacks[h]

    def plane(p, r):
        ref, start = (below, (12 + r) * chan_in) if p < 0 else (own, (4 * p + r) * chan_in)
        return ref[start : start + chan_in, :]

    blank = jnp.zeros((chan_in, cells), BF)
    lefts = []
    for a in range(3):
        for b in range(3):
            pieces = []
            for i in range(2):
                for j in range(2):
                    r = 2 * j + b - 1
                    pieces.append(blank if r < 0 else plane(2 * i + a - 1, r))
            lefts.append(jnp.concatenate(pieces, 1))
    result = dot_rows(jnp.concatenate(lefts, 0), jnp.concatenate(stacks[:2], 1))
    for ab in range(9):
        for e in range(3):
            start = (3 * ab + e) * chan_in
            grads[start : start + chan_in, :] = result[
                ab * chan_in : (ab + 1) * chan_in, e * chan : (e + 1) * chan
            ]
    grads[27 * chan_in :, :] = jnp.zeros((chan_in, chan), F32)
    samples_n, size = kept_ref.shape[:2]
    for m in range(samples_n):
        lower = grads[2 * m * size : (2 * m + 1) * size, :]
        upper = grads[(2 * m + 1) * size : (2 * m + 2) * size, :]
        kept_ref[m] = jnp.where(parity == 0, lower, upper).astype(BF)
        sent_ref[m] = jnp.where(parity == 0, upper, lower).astype(BF)


def middle_kernel(mine, theirs, stacks, first_weight, second_ref, volume_ref):
    chan_in, cells = volume_ref.shape[2:]
    chan = second_ref.shape[2]
    def filters(a):
        return [
            jnp.concatenate([first_weight[9 * a + 3 * b + e] for e in range(3)], 1) for b in range(3)
        ]

    totals = {}
    for h, chosen in enumerate(((1, 2), (0, 1, 2), (0,))):
        left = jnp.concatenate(sum([filters(a) for a in chosen], []), 0)
        result = dot(left, stacks[h])
        for place, a in enumerate(chosen):
            p = 2 * h + a - 1
            for b in range(3):
                for j in range(2):
                    r = 2 * j + b - 1
                    if r < 0:
                        continue
                    start = (3 * place + b) * chan_in
                    term = result[start : start + chan_in, j * cells : (j + 1) * cells]
                    totals[p, r] = totals[p, r] + term if (p, r) in totals else term
    for (p, r), total in totals.items():
        volume_ref[p, r] = total.astype(BF)

    share = 5 * chan
    both = jnp.concatenate([mine[...], theirs[...]], 0)
    second = lax.dot_general(
        both[:, share:], both[:, :share], (((0,), (0,)), ((), ())), preferred_element_type=F32
    ).astype(BF)
    per = 32 // second_ref.shape[0]
    for piece in range(32):
        m, at = piece // per, piece % per * 40
        first = piece // 2 * 16
        for lane in range(2, 5) if piece % 2 else range(3):
            begin = first + 8 if lane == 2 and piece % 2 else first
            count = 8 if lane == 2 else 16
            second_ref[m, at : at + count, :] = second[
                begin : begin + count, lane * chan : (lane + 1) * chan
            ]
            at += count


def pack_kernel(second, kept, got, payload_ref):
    rows = second.shape[1]
    for m in range(kept.shape[0]):
        payload_ref[m, :rows, :] = second[m]
        total = kept[m].astype(F32) + got[m].astype(F32)
        payload_ref[m, rows:, :] = total.astype(BF)


def final_kernel(chunks, first_ref, second_ref):
    taps, chan_in, chan = first_ref.shape
    samples_n, rows = chunks.shape[0], chunks.shape[1] - 12
    for m in range(samples_n):
        lines = chunks[m].astype(F32)[12:].astype(BF)
        at, stop = m * rows, min((m + 1) * rows, taps * chan_in)
        while at < stop:
            tap, channel = at // chan_in, at % chan_in
            count = min(stop - at, chan_in - channel)
            begin = at - m * rows
            first_ref[tap, channel : channel + count, :] = lines[begin : begin + count]
            at += count
    per_group = second_ref.shape[1]

    def test(r, c):
        tap, o = r >> 4, r & 15
        q = jnp.where(tap >= 9, 1, 0)
        w = jnp.where(tap - 9 * q >= 5, 1, 0)
        block = tap - 9 * q - 4 * w - 2 * ((c >> 4) & 1)
        right = (block >= 0) & (block <= 2) & ((c & 15) == 6 * w + 3 * q + block)
        return right & ((c >> 5) == o)

    parts = jnp.concatenate([chunks[m, :16, :] for m in range(samples_n)], 0)
    live = dot(picker(18 * per_group, 16 * samples_n, test), parts).astype(BF)
    for a in range(3):
        for b in range(9):
            tap = 6 * a + b - 3
            value = live[tap * per_group : (tap + 1) * per_group]
            second_ref[9 * a + b] = jnp.zeros((per_group, chan), BF) if b < 3 else value


def exchanged(parts, axis):
    return lax.all_to_all(parts, axis, split_axis=0, concat_axis=0, tiled=True)


def everywhere(value, axis):
    return exchanged(jnp.broadcast_to(value[None], (lax.axis_size(axis),) + value.shape), axis)


def shards(input_field, out_cotangent, first_weight, second_weight):
    chan_in, planes, height, length = input_field.shape[1:]
    chan_mid, chan_out = second_weight.shape[1:]
    groups = lax.axis_size("space")
    samples_n = lax.axis_size("sample")
    rows, half, quarter = (height // 2, length // 2, length // 4)
    per_group = chan_out // groups
    own = input_field[0].transpose(1, 2, 0, 3).reshape(-1, length)
    cotangent = out_cotangent[0].reshape(chan_out, quarter).T.reshape(4, 8, 2, 128)
    own = jnp.concatenate([own, cotangent.transpose(0, 2, 1, 3).reshape(64, 128)], 0)
    above = lax.ppermute(own, "space", [(i, (i - 1) % groups) for i in range(groups)])
    below = lax.ppermute(own, "space", [(i, i + 1) for i in range(groups - 1)])
    flipped = first_weight.reshape(27 * chan_in, chan_mid).T
    flat_second = second_weight.reshape(27 * chan_mid, chan_out)
    place = lax.axis_index("space")
    marks = [place % 2, jnp.where(place == groups - 1, 0, 1), place // 2 % 2]
    index = jnp.arange(3)
    scalars = jnp.where(index == 0, marks[0], jnp.where(index == 1, marks[1], marks[2]))
    scalars = scalars.astype(jnp.int32)
    size = 14 * chan_in // samples_n
    per = 32 // samples_n
    smem = pl.BlockSpec(memory_space=pltpu.SMEM)
    vmem = pl.BlockSpec(memory_space=pltpu.VMEM)
    swapped = jax.ShapeDtypeStruct((2 * quarter, 5 * chan_mid + chan_out), BF)
    halved = jax.ShapeDtypeStruct((samples_n, size, chan_mid), BF)
    pre, delta, mine, theirs = pl.pallas_call(
        forward_kernel,
        out_shape=(
            jax.ShapeDtypeStruct((3, chan_mid, rows * half), F32),
            jax.ShapeDtypeStruct((chan_out, 2 * quarter), BF),
            swapped,
            swapped,
        ),
        in_specs=[smem] + [vmem] * 5,
        scratch_shapes=[
            pltpu.VMEM((27 * chan_in, 5 * rows * half), BF),
            pltpu.VMEM((2 * quarter, 18 * chan_mid), BF),
        ],
        compiler_params=pltpu.CompilerParams(vmem_limit_bytes=16 << 20),
        cost_estimate=pl.CostEstimate(
            flops=2_000_000_000, bytes_accessed=5_000_000, transcendentals=0
        ),
    )(scalars, below, own, above, flipped, flat_second)
    theirs = lax.ppermute(theirs, "space", [(i, i ^ 2) for i in range(groups)])
    stacks, kept, sent = pl.pallas_call(
        backward_kernel,
        out_shape=(jax.ShapeDtypeStruct((3, 3 * chan_mid, 2 * length), BF), halved, halved),
        in_specs=[smem] + [vmem] * 5,
        scratch_shapes=[pltpu.VMEM((28 * chan_in, chan_mid), F32)],
        compiler_params=pltpu.CompilerParams(vmem_limit_bytes=16 << 20),
        cost_estimate=pl.CostEstimate(
            flops=3_000_000_000, bytes_accessed=5_000_000, transcendentals=0
        ),
    )(scalars, below, own, delta, pre, flat_second)
    got = lax.ppermute(sent, "space", [(i, i ^ 1) for i in range(groups)])
    second, volume = pl.pallas_call(
        middle_kernel,
        out_shape=(
            jax.ShapeDtypeStruct((samples_n, per * 40, chan_mid), BF),
            jax.ShapeDtypeStruct((planes, height, chan_in, length), BF),
        ),
        compiler_params=pltpu.CompilerParams(vmem_limit_bytes=8 << 20),
        cost_estimate=pl.CostEstimate(
            flops=2_000_000_000, bytes_accessed=2_000_000, transcendentals=0
        ),
    )(mine, theirs, stacks, first_weight)
    payload = pl.pallas_call(
        pack_kernel,
        out_shape=jax.ShapeDtypeStruct((samples_n, per * 40 + size, chan_mid), BF),
        compiler_params=pltpu.CompilerParams(vmem_limit_bytes=8 << 20),
        cost_estimate=pl.CostEstimate(
            flops=50_000_000, bytes_accessed=2_000_000, transcendentals=0
        ),
    )(second, kept, got)
    input_grad = volume.transpose(2, 0, 1, 3)[None]
    chunk = jnp.sum(exchanged(payload, "sample").astype(F32), 0)
    first_chunk = jnp.broadcast_to(chunk[None, per * 40 :], (groups, size, chan_mid))
    second_chunk = chunk[: per * 40].reshape(per, 40, chan_mid)
    odd = (lax.axis_index("sample") * per + jnp.arange(per)) % 2 == 1
    second_chunk = jnp.where(
        odd[:, None, None],
        jnp.pad(second_chunk, ((0, 0), (8, 0), (0, 0))),
        jnp.pad(second_chunk, ((0, 0), (0, 8), (0, 0))),
    )
    pieces = 3 * per
    second_chunk = second_chunk.reshape(pieces, groups, chan_mid).transpose(1, 0, 2)
    second_chunk = jnp.pad(second_chunk, ((0, 0), (0, -(size + pieces) % 8), (0, 0)))
    both = exchanged(jnp.concatenate([first_chunk, second_chunk], 1).astype(BF), "space")
    both = both.astype(F32)
    first_chunk = jnp.sum(both[:, :size].reshape(groups // 2, 2, size, chan_mid), 0)
    second_chunk = both[:, size : size + pieces].reshape(groups // 4, 4, pieces, chan_mid)
    second_chunk = jnp.sum(second_chunk, 0)
    first_ext = planes // 2 * rows * half
    first_scale = 1.0 / math.sqrt(samples_n * groups * first_ext)
    second_scale = 1.0 / math.sqrt(samples_n * groups * (planes // 4) * (height // 4) * quarter)
    first_chunk = first_chunk.reshape(2 * size, chan_mid) * first_scale
    second_chunk = second_chunk.reshape(4 * pieces, chan_mid) * second_scale
    both = jnp.concatenate([second_chunk, first_chunk], 0).astype(BF)
    first_grad, second_grad = pl.pallas_call(
        final_kernel,
        out_shape=(
            jax.ShapeDtypeStruct((27, chan_in, chan_mid), BF),
            jax.ShapeDtypeStruct((27, per_group, chan_mid), BF),
        ),
        compiler_params=pltpu.CompilerParams(vmem_limit_bytes=8 << 20),
        cost_estimate=pl.CostEstimate(
            flops=40_000_000, bytes_accessed=1_200_000, transcendentals=0
        ),
    )(everywhere(both, "sample"))
    second_grad = second_grad.transpose(0, 2, 1)
    return input_grad, first_grad, second_grad


def solution(mesh):
    placed = (
        P("sample", None, "space", None, None),
        P("sample", None, "space", None, None),
        P(),
        P(),
    )
    return jax.shard_map(
        shards,
        mesh=mesh,
        in_specs=placed,
        out_specs=(P("sample", None, "space", None, None), P(), P(None, None, "space")),
        check_vma=False,
    )
```

```python
import math

import jax
import jax.numpy as jnp
from jax import lax
from jax.experimental import pallas as pl
from jax.experimental.pallas import tpu as pltpu
from jax.sharding import PartitionSpec as P

BF = jnp.bfloat16
F32 = jnp.float32


def gradient_silu(values):
    logistic = jax.nn.sigmoid(values)
    return logistic * (1.0 + values * (1.0 - logistic))


def dot(left, right):
    return jnp.dot(left, right, preferred_element_type=F32)


def dot_rows(left, right):
    return lax.dot_general(left, right, (((1,), (1,)), ((), ())), preferred_element_type=F32)


def picker(rows, columns, test):
    r = lax.broadcasted_iota(jnp.int32, (rows, columns), 0)
    c = lax.broadcasted_iota(jnp.int32, (rows, columns), 1)
    return jnp.where(test(r, c), 1.0, 0.0).astype(BF)


def down_first_test(r, c):
    return ((r >> 7) == ((c >> 6) & 1)) & ((r & 127) == 2 * (c & 63) + (c >> 7) - 1)


def up_first_test(r, c):
    return ((r >> 6) == ((c >> 7) & 1)) & ((c & 127) == 2 * (r & 63) + (c >> 8) - 1)


def down_second_test(r, c):
    be = r >> 5
    b = jnp.where(be >= 3, 1, 0)
    return (b == (c >> 6)) & ((c & 63) == 2 * (r & 31) + be - 3 * b - 1)


def up_second_test(r, c):
    ibe = c >> 7
    i = jnp.where(ibe >= 6, 1, 0)
    be = ibe - 6 * i
    b = jnp.where(be >= 3, 1, 0)
    return ((r >> 5) == i) & (b == ((c >> 6) & 1)) & ((c & 63) == 2 * (r & 31) + be - 3 * b - 1)


def reorder_test(r, c):
    return ((r >> 4) == (c & 15)) & ((r & 15) == (c >> 4))


def forward_kernel(
    scalars, below, own, above, flipped, second_weight,
    pre_ref, delta_ref, kept_ref, sent_ref, blocks, taps,
):
    parity, inside = scalars[0], scalars[1] > 0
    chan_in, cells = 64, 128
    group = 9 * chan_in
    down_first = picker(2 * cells, 3 * 128, down_first_test)
    down_second = picker(192, 128, down_second_test)
    first = 0
    for part, planes, skip in ((below, 3, 4), (own, 4, 0), (above, 4, 0)):

        def row(r):
            lines = [
                part[(4 * p + r + skip) * chan_in : (4 * p + r + skip + 1) * chan_in, :]
                for p in range(planes)
            ]
            return jnp.concatenate(lines, 0)

        for b in range(3):
            if b == 0:
                picked = dot(row(1), down_first[cells:, :])
            else:
                picked = dot(jnp.concatenate([row(b - 1), row(b + 1)], 1), down_first)
            picked = picked.astype(BF)
            for p in range(planes):
                for e in range(3):
                    value = picked[p * chan_in : (p + 1) * chan_in, e * 128 : (e + 1) * 128]
                    for a in range(3):
                        h, odd = (first + p - a) // 2, (first + p - a) % 2
                        if odd or not 0 <= h <= 4:
                            continue
                        placed = value
                        if (a, h) == (0, 3):
                            placed = jnp.where(inside, value.astype(F32), 0.0).astype(BF)
                        start = a * group + (3 * b + e) * chan_in
                        blocks[start : start + chan_in, h * 128 : (h + 1) * 128] = placed
        first += planes
    quarter = 32
    lines = 16 * chan_in
    cotangent = jnp.concatenate(
        [
            part[lines + 16 * tile + 8 * half : lines + 16 * tile + 8 * half + 8, :].astype(F32)
            for half in range(2)
            for part in (own, above)
            for tile in range(4)
        ],
        0,
    )
    cotangent = jnp.concatenate([cotangent[:64], cotangent[64:]], 1)
    pres = []
    wide = dot(flipped[...], blocks[...])
    for h in range(5):
        pre = wide[:, h * 128 : (h + 1) * 128]
        pres.append(pre)
        hidden = (pre * jax.nn.sigmoid(pre)).astype(BF)
        chan = hidden.shape[0]
        picked = dot_rows(down_second, hidden)
        for i in range(2):
            a = h - 2 * i
            if 0 <= a <= 2:
                masked = jnp.where(inside, picked, 0.0) if (i, a) == (1, 0) else picked
                masked = masked.astype(BF)
                for be in range(6):
                    taps[i * quarter : (i + 1) * quarter, (6 * a + be) * chan : (6 * a + be + 1) * chan] = (
                        masked[be * quarter : (be + 1) * quarter]
                    )
    pre = None
    for a in range(3):
        rows = second_weight[(9 * a + 3) * chan : 9 * (a + 1) * chan, :]
        term = dot(taps[:, 6 * a * chan : 6 * (a + 1) * chan], rows)
        pre = term if pre is None else pre + term
    ended = cotangent * gradient_silu(pre)
    delta = jnp.concatenate([ended[:quarter], jnp.where(inside, ended[quarter:], 0.0)], 0).T
    delta = delta.astype(BF)
    delta_ref[...] = delta
    for h in range(3):
        pre_ref[h] = pres[h + 1]
    share = 5 * chan
    ordered = dot(ended.astype(BF), picker(256, 256, reorder_test)).astype(BF)
    for ref, end in ((kept_ref, scalars[2]), (sent_ref, 1 - scalars[2])):
        start = pl.multiple_of((9 * parity + 4 * end) * chan, 128)
        ref[:, :share] = taps[:, pl.ds(start, share)]
        ref[:, share:] = ordered


def backward_kernel(
    scalars, below, own, delta_ref, pre_ref, second_weight,
    stacks_ref, kept_ref, sent_ref, grads,
):
    parity = scalars[0]
    chan_in, cells = 64, 128
    chan = pre_ref.shape[1]
    delta = delta_ref[...]
    up_first = picker(128, 768, up_first_test)
    up_second = picker(64, 1536, up_second_test)
    spread = dot(delta, up_second).astype(BF)
    lanes = spread.shape[1] // 12
    deltas = []
    for h, pairs in enumerate((((1, 0),), ((2, 0), (0, 1)), ((1, 1),))):
        total = None
        for a, i in pairs:
            for be in range(6):
                start = (9 * a + 3 + be) * chan
                term = dot(
                    second_weight[start : start + chan, :],
                    spread[:, (6 * i + be) * lanes : (6 * i + be + 1) * lanes],
                )
                total = term if total is None else total + term
        deltas.append((total * gradient_silu(pre_ref[h])).astype(BF))
    raised = dot(jnp.concatenate(deltas, 0), up_first).astype(BF)
    wide = 2 * cells
    stacks = [
        jnp.concatenate(
            [raised[h * chan : (h + 1) * chan, e * wide : (e + 1) * wide] for e in range(3)], 0
        )
        for h in range(3)
    ]

    for h in range(3):
        stacks_ref[h] = stacks[h]

    def plane(p, r):
        ref, start = (below, (12 + r) * chan_in) if p < 0 else (own, (4 * p + r) * chan_in)
        return ref[start : start + chan_in, :]

    blank = jnp.zeros((chan_in, cells), BF)
    lefts = []
    for a in range(3):
        for b in range(3):
            pieces = []
            for i in range(2):
                for j in range(2):
                    r = 2 * j + b - 1
                    pieces.append(blank if r < 0 else plane(2 * i + a - 1, r))
            lefts.append(jnp.concatenate(pieces, 1))
    result = dot_rows(jnp.concatenate(lefts, 0), jnp.concatenate(stacks[:2], 1))
    for ab in range(9):
        for e in range(3):
            start = (3 * ab + e) * chan_in
            grads[start : start + chan_in, :] = result[
                ab * chan_in : (ab + 1) * chan_in, e * chan : (e + 1) * chan
            ]
    grads[27 * chan_in :, :] = jnp.zeros((chan_in, chan), F32)
    samples_n, size = kept_ref.shape[:2]
    for m in range(samples_n):
        lower = grads[2 * m * size : (2 * m + 1) * size, :]
        upper = grads[(2 * m + 1) * size : (2 * m + 2) * size, :]
        kept_ref[m] = jnp.where(parity == 0, lower, upper).astype(BF)
        sent_ref[m] = jnp.where(parity == 0, upper, lower).astype(BF)


def middle_kernel(mine, theirs, stacks, first_weight, second_ref, volume_ref):
    chan_in, cells = volume_ref.shape[2:]
    chan = second_ref.shape[2]
    def filters(a):
        return [
            jnp.concatenate([first_weight[9 * a + 3 * b + e] for e in range(3)], 1) for b in range(3)
        ]

    totals = {}
    for h, chosen in enumerate(((1, 2), (0, 1, 2), (0,))):
        left = jnp.concatenate(sum([filters(a) for a in chosen], []), 0)
        result = dot(left, stacks[h])
        for place, a in enumerate(chosen):
            p = 2 * h + a - 1
            for b in range(3):
                for j in range(2):
                    r = 2 * j + b - 1
                    if r < 0:
                        continue
                    start = (3 * place + b) * chan_in
                    term = result[start : start + chan_in, j * cells : (j + 1) * cells]
                    totals[p, r] = totals[p, r] + term if (p, r) in totals else term
    for (p, r), total in totals.items():
        volume_ref[p, r] = total.astype(BF)

    share = 5 * chan
    both = jnp.concatenate([mine[...], theirs[...]], 0)
    second = lax.dot_general(
        both[:, share:], both[:, :share], (((0,), (0,)), ((), ())), preferred_element_type=F32
    ).astype(BF)
    per = 32 // second_ref.shape[0]
    for piece in range(32):
        m, at = piece // per, piece % per * 40
        first = piece // 2 * 16
        for lane in range(2, 5) if piece % 2 else range(3):
            begin = first + 8 if lane == 2 and piece % 2 else first
            count = 8 if lane == 2 else 16
            second_ref[m, at : at + count, :] = second[
                begin : begin + count, lane * chan : (lane + 1) * chan
            ]
            at += count


def pack_kernel(second, kept, got, payload_ref):
    rows = second.shape[1]
    for m in range(kept.shape[0]):
        payload_ref[m, :rows, :] = second[m]
        payload_ref[m, rows:, :] = kept[m] + got[m]


def final_kernel(chunks, first_ref, second_ref):
    taps, chan_in, chan = first_ref.shape
    samples_n, rows = chunks.shape[0], chunks.shape[1] - 12
    for m in range(samples_n):
        lines = chunks[m].astype(F32)[12:].astype(BF)
        at, stop = m * rows, min((m + 1) * rows, taps * chan_in)
        while at < stop:
            tap, channel = at // chan_in, at % chan_in
            count = min(stop - at, chan_in - channel)
            begin = at - m * rows
            first_ref[tap, channel : channel + count, :] = lines[begin : begin + count]
            at += count
    per_group = second_ref.shape[1]

    def test(r, c):
        tap, o = r >> 4, r & 15
        q = jnp.where(tap >= 9, 1, 0)
        w = jnp.where(tap - 9 * q >= 5, 1, 0)
        block = tap - 9 * q - 4 * w - 2 * ((c >> 4) & 1)
        right = (block >= 0) & (block <= 2) & ((c & 15) == 6 * w + 3 * q + block)
        return right & ((c >> 5) == o)

    parts = jnp.concatenate([chunks[m, :16, :] for m in range(samples_n)], 0)
    live = dot(picker(18 * per_group, 16 * samples_n, test), parts).astype(BF)
    for a in range(3):
        for b in range(9):
            tap = 6 * a + b - 3
            value = live[tap * per_group : (tap + 1) * per_group]
            second_ref[9 * a + b] = jnp.zeros((per_group, chan), BF) if b < 3 else value


def exchanged(parts, axis):
    return lax.all_to_all(parts, axis, split_axis=0, concat_axis=0, tiled=True)


def everywhere(value, axis):
    return exchanged(jnp.broadcast_to(value[None], (lax.axis_size(axis),) + value.shape), axis)


def shards(input_field, out_cotangent, first_weight, second_weight):
    chan_in, planes, height, length = input_field.shape[1:]
    chan_mid, chan_out = second_weight.shape[1:]
    groups = lax.axis_size("space")
    samples_n = lax.axis_size("sample")
    rows, half, quarter = (height // 2, length // 2, length // 4)
    per_group = chan_out // groups
    own = input_field[0].transpose(1, 2, 0, 3).reshape(-1, length)
    cotangent = out_cotangent[0].reshape(chan_out, quarter).T.reshape(4, 8, 2, 128)
    own = jnp.concatenate([own, cotangent.transpose(0, 2, 1, 3).reshape(64, 128)], 0)
    above = lax.ppermute(own, "space", [(i, (i - 1) % groups) for i in range(groups)])
    below = lax.ppermute(own, "space", [(i, i + 1) for i in range(groups - 1)])
    flipped = first_weight.reshape(27 * chan_in, chan_mid).T
    flat_second = second_weight.reshape(27 * chan_mid, chan_out)
    place = lax.axis_index("space")
    marks = [place % 2, jnp.where(place == groups - 1, 0, 1), place // 2 % 2]
    index = jnp.arange(3)
    scalars = jnp.where(index == 0, marks[0], jnp.where(index == 1, marks[1], marks[2]))
    scalars = scalars.astype(jnp.int32)
    size = 14 * chan_in // samples_n
    per = 32 // samples_n
    smem = pl.BlockSpec(memory_space=pltpu.SMEM)
    vmem = pl.BlockSpec(memory_space=pltpu.VMEM)
    swapped = jax.ShapeDtypeStruct((2 * quarter, 5 * chan_mid + chan_out), BF)
    halved = jax.ShapeDtypeStruct((samples_n, size, chan_mid), BF)
    pre, delta, mine, theirs = pl.pallas_call(
        forward_kernel,
        out_shape=(
            jax.ShapeDtypeStruct((3, chan_mid, rows * half), F32),
            jax.ShapeDtypeStruct((chan_out, 2 * quarter), BF),
            swapped,
            swapped,
        ),
        in_specs=[smem] + [vmem] * 5,
        scratch_shapes=[
            pltpu.VMEM((27 * chan_in, 5 * rows * half), BF),
            pltpu.VMEM((2 * quarter, 18 * chan_mid), BF),
        ],
        compiler_params=pltpu.CompilerParams(vmem_limit_bytes=16 << 20),
        cost_estimate=pl.CostEstimate(
            flops=2_000_000_000, bytes_accessed=5_000_000, transcendentals=0
        ),
    )(scalars, below, own, above, flipped, flat_second)
    theirs = lax.ppermute(theirs, "space", [(i, i ^ 2) for i in range(groups)])
    stacks, kept, sent = pl.pallas_call(
        backward_kernel,
        out_shape=(jax.ShapeDtypeStruct((3, 3 * chan_mid, 2 * length), BF), halved, halved),
        in_specs=[smem] + [vmem] * 5,
        scratch_shapes=[pltpu.VMEM((28 * chan_in, chan_mid), F32)],
        compiler_params=pltpu.CompilerParams(vmem_limit_bytes=16 << 20),
        cost_estimate=pl.CostEstimate(
            flops=3_000_000_000, bytes_accessed=5_000_000, transcendentals=0
        ),
    )(scalars, below, own, delta, pre, flat_second)
    got = lax.ppermute(sent, "space", [(i, i ^ 1) for i in range(groups)])
    second, volume = pl.pallas_call(
        middle_kernel,
        out_shape=(
            jax.ShapeDtypeStruct((samples_n, per * 40, chan_mid), BF),
            jax.ShapeDtypeStruct((planes, height, chan_in, length), BF),
        ),
        compiler_params=pltpu.CompilerParams(vmem_limit_bytes=8 << 20),
        cost_estimate=pl.CostEstimate(
            flops=2_000_000_000, bytes_accessed=2_000_000, transcendentals=0
        ),
    )(mine, theirs, stacks, first_weight)
    payload = pl.pallas_call(
        pack_kernel,
        out_shape=jax.ShapeDtypeStruct((samples_n, per * 40 + size, chan_mid), BF),
        compiler_params=pltpu.CompilerParams(vmem_limit_bytes=8 << 20),
        cost_estimate=pl.CostEstimate(
            flops=50_000_000, bytes_accessed=2_000_000, transcendentals=0
        ),
    )(second, kept, got)
    input_grad = volume.transpose(2, 0, 1, 3)[None]
    chunk = jnp.sum(exchanged(payload, "sample").astype(F32), 0)
    first_chunk = jnp.broadcast_to(chunk[None, per * 40 :], (groups, size, chan_mid))
    second_chunk = chunk[: per * 40].reshape(per, 40, chan_mid)
    odd = (lax.axis_index("sample") * per + jnp.arange(per)) % 2 == 1
    second_chunk = jnp.where(
        odd[:, None, None],
        jnp.pad(second_chunk, ((0, 0), (8, 0), (0, 0))),
        jnp.pad(second_chunk, ((0, 0), (0, 8), (0, 0))),
    )
    pieces = 3 * per
    second_chunk = second_chunk.reshape(pieces, groups, chan_mid).transpose(1, 0, 2)
    second_chunk = jnp.pad(second_chunk, ((0, 0), (0, -(size + pieces) % 8), (0, 0)))
    both = exchanged(jnp.concatenate([first_chunk, second_chunk], 1).astype(BF), "space")
    both = both.astype(F32)
    first_chunk = jnp.sum(both[:, :size].reshape(groups // 2, 2, size, chan_mid), 0)
    second_chunk = both[:, size : size + pieces].reshape(groups // 4, 4, pieces, chan_mid)
    second_chunk = jnp.sum(second_chunk, 0)
    first_ext = planes // 2 * rows * half
    first_scale = 1.0 / math.sqrt(samples_n * groups * first_ext)
    second_scale = 1.0 / math.sqrt(samples_n * groups * (planes // 4) * (height // 4) * quarter)
    first_chunk = first_chunk.reshape(2 * size, chan_mid) * first_scale
    second_chunk = second_chunk.reshape(4 * pieces, chan_mid) * second_scale
    both = jnp.concatenate([second_chunk, first_chunk], 0).astype(BF)
    first_grad, second_grad = pl.pallas_call(
        final_kernel,
        out_shape=(
            jax.ShapeDtypeStruct((27, chan_in, chan_mid), BF),
            jax.ShapeDtypeStruct((27, per_group, chan_mid), BF),
        ),
        compiler_params=pltpu.CompilerParams(vmem_limit_bytes=8 << 20),
        cost_estimate=pl.CostEstimate(
            flops=40_000_000, bytes_accessed=1_200_000, transcendentals=0
        ),
    )(everywhere(both, "sample"))
    second_grad = second_grad.transpose(0, 2, 1)
    return input_grad, first_grad, second_grad


def solution(mesh):
    placed = (
        P("sample", None, "space", None, None),
        P("sample", None, "space", None, None),
        P(),
        P(),
    )
    return jax.shard_map(
        shards,
        mesh=mesh,
        in_specs=placed,
        out_specs=(P("sample", None, "space", None, None), P(), P(None, None, "space")),
        check_vma=False,
    )
```
